128 devices in a mesh: blk: 8 (over x_lo, y), head: 8 (over z, core), grp: 2 (over x_hi).
Axes of the slice: x: 4 (x_hi: 2, x_lo: 2; x = x_hi * 2 + x_lo), y: 4, z: 4, core: 2. Of those that a mesh axis runs over, the one named last changes fastest.
Arguments:
- t_query: bfloat16 [8192, 4096], P('blk', ('head', 'grp')), may hold values from -80 to 80
- t_key: bfloat16 [8192, 4096], P('blk', ('head', 'grp')), may hold values from -80 to 80
- t_value: bfloat16 [8192, 4096], P('blk', ('head', 'grp')), may hold values from -6 to 6
- t_out: bfloat16 [4096, 4096], P(('head', 'grp')), may hold values from -0.09375 to 0.09375
- s_query: bfloat16 [8192, 2048], P('blk', ('head', 'grp')), may hold values from -80 to 80
- s_key: bfloat16 [8192, 2048], P('blk', ('head', 'grp')), may hold values from -80 to 80
- s_value: bfloat16 [8192, 2048], P('blk', ('head', 'grp')), may hold values from -6 to 6
- s_out: bfloat16 [2048, 4096], P(('head', 'grp')), may hold values from -0.125 to 0.125
- segments: int32 [8192], P('blk'), may hold values from 0 to 1, never falling along the last dimension, each value on 1 to 8128 neighbouring positions
- selection: int32 [128, 16], P('blk'), may hold values from 0 to 127, as said below
Outputs:
- mismatch: float32 [8192, 4096], P('blk', ('head', 'grp'))
- s_dq: float32 [8192, 2048], P('blk', ('head', 'grp'))
- s_dk: float32 [8192, 2048], P('blk', ('head', 'grp'))
- s_dv: float32 [8192, 2048], P('blk', ('head', 'grp'))
The draws below stay inside these ranges and needn't reach their ends.
Inputs may be any that keep to these rules, and one draw needn't show every extreme that they name: `selection`: entry 0 of row b is b itself; for b >= 64, entry 1 of row b is b - 64; every entry of row b lies between 0 and b; entries of a row may repeat. `segments`: document numbers never fall along the sequence.
All inputs are finite; a program needn't handle non-finite values.
Results may differ from the reference program's by a relative error of at most 0.015.
Values may be sent and summed in bfloat16 or wider, within the bound.
No kernel may reach another device: no remote copies, remote signals or barrier semaphores. Data moves between devices by JAX's collectives and lax.ppermute only.
A program may use at most 128 MiB of HBM per device.

```python
import math
import jax
import jax.numpy as jnp
import numpy as np
from jax import lax

D = 4096
TH = 32
SH = 16
HD = 128
BS = 64
NSEL = 16
TOKENS = 8192
N_HEAD = 8
N_GRP = 2


def drawn_pair(key, columns, salt):
    folded = jax.random.fold_in(key, salt)
    key_rows = jax.random.normal(jax.random.fold_in(folded, 1), (TOKENS, columns), jnp.float32)
    queries = 2.5 * jax.random.normal(jax.random.fold_in(folded, 2), (TOKENS, columns), jnp.float32)
    return (queries.astype(jnp.bfloat16), key_rows.astype(jnp.bfloat16))


def draw_t_query(key, part):
    return drawn_pair(key, TH * HD, 101)[0]


def draw_t_key(key, part):
    return drawn_pair(key, TH * HD, 101)[1]


def draw_s_query(key, part):
    return drawn_pair(key, SH * HD, 202)[0]


def draw_s_key(key, part):
    return drawn_pair(key, SH * HD, 202)[1]


def draw_selection(key, part):
    block_count = TOKENS // BS
    rows = jnp.arange(block_count, dtype=jnp.int32)
    upper_bound = rows[:, None] + 1
    first_back = jax.random.randint(jax.random.fold_in(key, 303), (block_count, NSEL), 0, upper_bound, dtype=jnp.int32)
    second_back = jax.random.randint(jax.random.fold_in(key, 304), (block_count, NSEL), 0, upper_bound, dtype=jnp.int32)
    chosen = (rows[:, None] - jnp.minimum(first_back, second_back)).astype(jnp.int32)
    half = block_count // 2
    far_block = jnp.where(rows >= half, rows - half, chosen[:, 1]).astype(jnp.int32)
    chosen = chosen.at[:, 1].set(far_block)
    return chosen.at[:, 0].set(rows).astype(jnp.int32)


def shard_levels(stream_key, extent, split, low, high):
    loudness = 1.0
    for axis_at, parts in split:
        heights = jax.random.uniform(jax.random.fold_in(jax.random.fold_in(stream_key, 6), axis_at), (parts,), jnp.float32, low / len(split), high / len(split))
        loudness = loudness * jnp.repeat(jnp.exp(heights), extent[axis_at] // parts).reshape((-1,) + (1,) * (len(extent) - 1 - axis_at))
    return loudness


def length_profile(count, total, reach, skew):
    portions = [(1 << 20) // math.isqrt(grade ** skew) + 1 for grade in range(2, count + 1)]
    surplus, holding = total - reach - (count - 1), [1] * (count - 1)
    while surplus > 0:
        movable = [i for i in range(count - 1) if holding[i] < reach]
        pool, remaining = sum([portions[i] for i in movable]), surplus
        for i in movable:
            extra = min(reach - holding[i], max(1, remaining * portions[i] // pool), surplus)
            holding[i] = holding[i] + extra
            surplus = surplus - extra
    return np.array([reach] + holding)


def uneven_parts(own_key, number_of, total, reach, lean):
    if number_of == 2:
        one = jax.random.randint(own_key, (), max(1, total - reach), min(reach, total - 1) + 1)
        return jnp.stack([one, total - one])
    lengths = jnp.asarray(length_profile(number_of, total, reach, lean), jnp.int32)
    couples = (number_of - 1) // 2
    donor, taker = lengths[1:1 + 2 * couples:2], lengths[2:2 + 2 * couples:2]
    room = jnp.minimum(donor - 1, reach - taker)
    passed = jax.random.randint(jax.random.fold_in(own_key, 1), (couples,), 0, 1 << 20) % (room + 1)
    lengths = lengths.at[1:1 + 2 * couples:2].set(donor - passed).at[2:2 + 2 * couples:2].set(taker + passed)
    return lengths[jax.random.permutation(jax.random.fold_in(own_key, 2), number_of)]


def normal_values(own_key, shape, deviation, reach, cuts=(), kind=jnp.bfloat16):
    array = deviation * jax.random.normal(own_key, shape, jnp.float32)
    if cuts:
        array = array * shard_levels(own_key, shape, cuts, -0.22, 0.18)
    return jnp.clip(array, -reach, reach).astype(kind)


def setup_inputs(seed: int = 0) -> dict:
    splits = jax.random.split(jax.random.key(seed), 11)
    return {
        "t_query": draw_t_query(jax.random.fold_in(splits[10], 71), 0),
        "t_key": draw_t_key(jax.random.fold_in(splits[10], 71), 0),
        "t_value": normal_values(splits[2], (TOKENS, TH * HD), 1.0, 6.0, ((0, 8), (1, 16))),
        "t_out": normal_values(splits[3], (TH * HD, D), (TH * HD) ** -0.5, 0.09375, ((0, 16),)),
        "s_query": draw_s_query(jax.random.fold_in(splits[10], 71), 0),
        "s_key": draw_s_key(jax.random.fold_in(splits[10], 71), 0),
        "s_value": normal_values(splits[6], (TOKENS, SH * HD), 1.0, 6.0, ((0, 8), (1, 16))),
        "s_out": normal_values(splits[7], (SH * HD, D), (SH * HD) ** -0.5, 0.125, ((0, 16),)),
        "segments": jnp.searchsorted(jnp.cumsum(uneven_parts(splits[8], 2, TOKENS, TOKENS - BS, 0)), jnp.arange(TOKENS), side="right").astype(jnp.int32),
        "selection": draw_selection(jax.random.fold_in(splits[10], 71), 0),
    }


masked_score = -1e+30

def teacher_head(queries, key_rows, value_rows, segment_all):
    positions = jnp.arange(queries.shape[0]).astype(jnp.int32)
    scores = jnp.dot(queries, key_rows.T, preferred_element_type=jnp.float32) * HD ** (-0.5)
    allowed = (positions[None, :] <= positions[:, None]) & (segment_all[None, :] == segment_all[:, None])
    scores = jnp.where(allowed, scores, masked_score)
    largest = lax.optimization_barrier(jnp.max(scores, axis=1, keepdims=True))
    weights = jnp.where(allowed, jnp.exp(scores - largest), 0.0)
    running = lax.optimization_barrier(jnp.sum(weights, axis=1, keepdims=True))
    blended = jnp.dot(weights.astype(jnp.bfloat16), value_rows, preferred_element_type=jnp.float32)
    return (blended / running).astype(jnp.bfloat16)

def student_attn(queries, key_all, value_all, segment_all, selection, first_row):
    row_count = queries.shape[0]
    head_count = queries.shape[1] // HD
    blocks = row_count // BS
    query_blocks = queries.reshape(blocks, BS, head_count, HD)
    key_blocks = key_all.reshape(-1, BS, head_count, HD)[selection].reshape(blocks, NSEL * BS, head_count, HD)
    value_blocks = value_all.reshape(-1, BS, head_count, HD)[selection].reshape(blocks, NSEL * BS, head_count, HD)
    key_pos = (selection[:, :, None] * BS + jnp.arange(BS).astype(jnp.int32)[None, None, :]).astype(jnp.int32).reshape(blocks, NSEL * BS)
    query_pos = (first_row + jnp.arange(row_count).astype(jnp.int32)).astype(jnp.int32).reshape(blocks, BS)
    key_seg = segment_all[key_pos]
    query_seg = segment_all[query_pos]
    scores = jnp.einsum('bqhd,bkhd->bhqk', query_blocks, key_blocks, precision=lax.Precision.HIGHEST) * HD ** (-0.5)
    allowed = ((key_pos[:, None, :] <= query_pos[:, :, None]) & (key_seg[:, None, :] == query_seg[:, :, None]))[:, None]
    scores = jnp.where(allowed, scores, masked_score)
    largest = lax.stop_gradient(lax.optimization_barrier(jnp.max(scores, axis=3, keepdims=True)))
    weights = jnp.where(allowed, jnp.exp(scores - largest), 0.0)
    weights = weights / lax.optimization_barrier(jnp.sum(weights, axis=3, keepdims=True))
    blended = jnp.einsum('bhqk,bkhd->bqhd', weights, value_blocks, precision=lax.Precision.HIGHEST)
    return blended.reshape(row_count, head_count * HD)

def reference(t_query, t_key, t_value, t_out, s_query, s_key, s_value, s_out, segments, selection):
    tokens = t_query.shape[0]

    def heads_first(matrix):
        return matrix.reshape(tokens, -1, HD).transpose(1, 0, 2)

    def heads_last(matrix):
        return matrix.transpose(1, 0, 2).reshape(tokens, -1)
    teacher = lax.map(lambda triple: teacher_head(triple[0], triple[1], triple[2], segments), (heads_first(t_query), heads_first(t_key), heads_first(t_value)))
    t_attn = heads_last(teacher)
    student_inputs = (heads_first(s_query.astype(jnp.float32)), heads_first(s_key.astype(jnp.float32)), heads_first(s_value.astype(jnp.float32)))

    def student_forward(triple):
        return student_attn(triple[0], triple[1], triple[2], segments, selection, 0)
    s_attn = heads_last(lax.map(student_forward, student_inputs)).astype(jnp.bfloat16)
    groups = N_HEAD * N_GRP
    teacher_cols = TH * HD // groups
    student_cols = SH * HD // groups
    mismatch = jnp.zeros((tokens, D), jnp.float32)
    for group_index in range(groups):
        student_part = jnp.dot(s_attn[:, group_index * student_cols:(group_index + 1) * student_cols], s_out[group_index * student_cols:(group_index + 1) * student_cols], preferred_element_type=jnp.float32)
        teacher_part = jnp.dot(t_attn[:, group_index * teacher_cols:(group_index + 1) * teacher_cols], t_out[group_index * teacher_cols:(group_index + 1) * teacher_cols], preferred_element_type=jnp.float32)
        rounded = lax.optimization_barrier((student_part - teacher_part).astype(jnp.bfloat16))
        mismatch = mismatch + rounded.astype(jnp.float32)
    grad_out = jnp.dot(mismatch.astype(jnp.bfloat16), s_out.T, preferred_element_type=jnp.float32)

    def student_backward(quadruple):

        def local_attn(first, second, third):
            return student_attn(first, second, third, segments, selection, 0)
        _, pullback = jax.vjp(local_attn, quadruple[0], quadruple[1], quadruple[2])
        return pullback(quadruple[3])
    grad_query, grad_keys, grad_values = lax.map(student_backward, student_inputs + (heads_first(grad_out),))
    return (mismatch, heads_last(grad_query), heads_last(grad_keys), heads_last(grad_values))
```

```python
import jax
import jax.numpy as jnp
from jax import lax
from jax.experimental import pallas as pl
from jax.experimental.pallas import tpu as pltpu
from jax.sharding import Mesh
from jax.sharding import PartitionSpec as P

HD = 128
BS = 64
NSEL = 16
BLOCK = 1024
TILE_Q = 512
TILE_K = 512
SCALE = HD ** (-0.5)
EXP_SCALE = SCALE * 1.4426950408889634
LOWEST = -1e30

BLK = ("xlo", "y")
GROUP = ("z", "core", "xhi")
ZX = ("z", "xhi")
f32 = jnp.float32
bf16 = jnp.bfloat16

SMEM = pltpu.SMEM
ROWS_NT = (((1,), (1,)), ((), ()))
ROWS_TN = (((0,), (0,)), ((), ()))


def y_pairs(shift, all_x, causal_x):
    pairs = []
    for x in range(2):
        for y in range(4):
            to = (y + shift) % 4
            if x in all_x or (x in causal_x and y < to):
                pairs.append((4 * x + y, 4 * x + to))
    return pairs


def place(meta, kv_refs, key_all, value_all):
    for j, ref in enumerate(kv_refs):
        start = pl.multiple_of(meta[8 + j] * BLOCK, BLOCK)
        key_all[pl.ds(start, BLOCK), :] = ref[:BLOCK, :]
        value_all[pl.ds(start, BLOCK), :] = ref[BLOCK : 2 * BLOCK, :]


def find_border(kv_refs, border_ref):
    counts = None
    for ref in kv_refs:
        part = ref[2 * BLOCK :, :].astype(f32)
        counts = part if counts is None else counts + part
    border_ref[0] = jnp.sum(counts).astype(jnp.int32)


def teacher_kernel(meta, q_ref, *refs):
    kv_refs, o_ref, key_all, value_all, border_ref = refs[:8], *refs[8:]
    step = pl.program_id(0)

    @pl.when(step == 0)
    def _():
        place(meta, kv_refs, key_all, value_all)
        find_border(kv_refs, border_ref)

    first = meta[0] * BLOCK + step * TILE_Q
    border = border_ref[0]
    low_first = jnp.where(first >= border, border, 0)
    low_last = jnp.where(first + TILE_Q - 1 >= border, border, 0)
    queries = q_ref[...]
    q_pos = first + lax.broadcasted_iota(jnp.int32, (TILE_Q, 1), 0)
    q_low = jnp.where(q_pos >= border, border, 0)

    def turn(masked, j, carry):
        largest, total, acc = carry
        start = pl.multiple_of(j * TILE_K, TILE_K)
        scores = lax.dot_general(
            queries, key_all[pl.ds(start, TILE_K), :], ROWS_NT, preferred_element_type=f32
        )
        if masked:
            k_pos = start + lax.broadcasted_iota(jnp.int32, (1, TILE_K), 1)
            scores = jnp.where((k_pos <= q_pos) & (k_pos >= q_low), scores, LOWEST)
        new = jnp.maximum(largest, jnp.max(scores, axis=1, keepdims=True))
        factor = jnp.exp2((largest - new) * EXP_SCALE)
        weights = jnp.exp2((scores - new) * EXP_SCALE)
        total = factor * total + jnp.sum(weights, axis=1, keepdims=True)
        acc = factor * acc + jnp.dot(
            weights.astype(bf16), value_all[pl.ds(start, TILE_K), :], preferred_element_type=f32
        )
        return new, total, acc

    carry = (
        jnp.full((TILE_Q, 1), LOWEST, f32),
        jnp.zeros((TILE_Q, 1), f32),
        jnp.zeros((TILE_Q, HD), f32),
    )
    begin = low_first // TILE_K
    diagonal = first // TILE_K
    clear = jnp.minimum((low_last + TILE_K - 1) // TILE_K, diagonal)
    carry = lax.fori_loop(begin, clear, lambda j, c: turn(True, j, c), carry)
    carry = lax.fori_loop(clear, diagonal, lambda j, c: turn(False, j, c), carry)
    for j in range(max(TILE_Q // TILE_K, 1)):
        carry = turn(True, diagonal + j, carry)
    _, total, acc = carry
    o_ref[...] = (acc / total).astype(bf16)


def teacher_attention(meta, queries, kv_blocks):
    return pl.pallas_call(
        teacher_kernel,
        grid=(BLOCK // TILE_Q,),
        in_specs=[
            pl.BlockSpec(memory_space=SMEM),
            pl.BlockSpec((TILE_Q, HD), lambda i: (i, 0)),
        ]
        + [pl.BlockSpec(memory_space=pltpu.VMEM)] * 8,
        out_specs=pl.BlockSpec((TILE_Q, HD), lambda i: (i, 0)),
        out_shape=jax.ShapeDtypeStruct((BLOCK, HD), bf16),
        scratch_shapes=[pltpu.VMEM((8 * BLOCK, HD), bf16)] * 2 + [SMEM((1,), jnp.int32)],
        compiler_params=pltpu.CompilerParams(vmem_limit_bytes=40 << 20),
        cost_estimate=pl.CostEstimate(
            flops=4 * 4 * BLOCK * BLOCK * HD, bytes_accessed=5 << 20, transcendentals=5 * BLOCK * BLOCK
        ),
        name="teacher_attention",
    )(meta, queries, *kv_blocks)


def chosen_rows(sel, row, table):
    pieces = []
    for n in range(NSEL):
        start = pl.multiple_of(sel[row * NSEL + n] * BS, BS)
        pieces.append(table[pl.ds(start, BS), :])
    return jnp.concatenate(pieces, axis=0)


def student_forward_kernel(meta, sel, q_ref, kpos_ref, *refs):
    kv_refs, o_ref, p_ref, key_all, value_all, border_ref = refs[:8], *refs[8:]
    row = pl.program_id(0)

    @pl.when(row == 0)
    def _():
        place(meta, kv_refs, key_all, value_all)
        find_border(kv_refs, border_ref)

    border = border_ref[0]
    q_pos = meta[0] * BLOCK + row * BS + lax.broadcasted_iota(jnp.int32, (BS, 1), 0)
    q_low = jnp.where(q_pos >= border, border, 0)
    k_pos = kpos_ref[0]
    scores = lax.dot_general(
        q_ref[...], chosen_rows(sel, row, key_all), ROWS_NT, preferred_element_type=f32
    )
    scores = jnp.where((k_pos <= q_pos) & (k_pos >= q_low), scores, LOWEST)
    weights = jnp.exp2((scores - jnp.max(scores, axis=1, keepdims=True)) * EXP_SCALE)
    total = jnp.sum(weights, axis=1, keepdims=True)
    p_ref[...] = weights / total
    blended = jnp.dot(
        weights.astype(bf16), chosen_rows(sel, row, value_all), preferred_element_type=f32
    )
    o_ref[...] = (blended / total).astype(bf16)


def student_forward(meta, sel, queries, k_pos, kv_blocks):
    rows = BLOCK // BS
    return pl.pallas_call(
        student_forward_kernel,
        grid=(rows,),
        in_specs=[
            pl.BlockSpec(memory_space=SMEM),
            pl.BlockSpec(memory_space=SMEM),
            pl.BlockSpec((BS, HD), lambda i: (i, 0)),
            pl.BlockSpec((1, 1, NSEL * BS), lambda i: (i, 0, 0)),
        ]
        + [pl.BlockSpec(memory_space=pltpu.VMEM)] * 8,
        out_specs=[
            pl.BlockSpec((BS, HD), lambda i: (i, 0)),
            pl.BlockSpec((BS, NSEL * BS), lambda i: (i, 0)),
        ],
        out_shape=[
            jax.ShapeDtypeStruct((BLOCK, HD), bf16),
            jax.ShapeDtypeStruct((BLOCK, NSEL * BS), f32),
        ],
        scratch_shapes=[pltpu.VMEM((8 * BLOCK, HD), bf16)] * 2 + [SMEM((1,), jnp.int32)],
        compiler_params=pltpu.CompilerParams(vmem_limit_bytes=40 << 20),
        cost_estimate=pl.CostEstimate(
            flops=4 * BLOCK * NSEL * BS * HD, bytes_accessed=9 << 20, transcendentals=BLOCK * NSEL * BS
        ),
        name="student_forward",
    )(meta, sel, queries, k_pos, *kv_blocks)


def student_backward_kernel(meta, sel, q_ref, p_ref, g_ref, *refs):
    kv_refs, dq_ref, out_refs = refs[:8], refs[8], refs[9:17]
    key_all, value_all, dk_all, dv_all = refs[17:]
    row = pl.program_id(0)

    @pl.when(row == 0)
    def _():
        place(meta, kv_refs, key_all, value_all)
        dk_all[...] = jnp.zeros_like(dk_all)
        dv_all[...] = jnp.zeros_like(dv_all)

    grad = jnp.sum(g_ref[...].astype(f32), axis=0).astype(bf16)
    weights = p_ref[...]
    weight_grad = lax.dot_general(
        grad, chosen_rows(sel, row, value_all), ROWS_NT, preferred_element_type=f32
    )
    row_dots = jnp.sum(weights * weight_grad, axis=1, keepdims=True)
    score_grad = (weights * (weight_grad - row_dots) * SCALE).astype(bf16)
    dq_ref[...] = jnp.dot(score_grad, chosen_rows(sel, row, key_all), preferred_element_type=f32)
    key_grad = lax.dot_general(score_grad, q_ref[...], ROWS_TN, preferred_element_type=f32)
    value_grad = lax.dot_general(weights.astype(bf16), grad, ROWS_TN, preferred_element_type=f32)
    for n in range(NSEL):
        start = pl.multiple_of(sel[row * NSEL + n] * BS, BS)
        dk_all[pl.ds(start, BS), :] += key_grad[n * BS : (n + 1) * BS, :]
        dv_all[pl.ds(start, BS), :] += value_grad[n * BS : (n + 1) * BS, :]

    @pl.when(row == pl.num_programs(0) - 1)
    def _():
        for j, ref in enumerate(out_refs):
            start = pl.multiple_of(meta[16 + j] * BLOCK, BLOCK)
            ref[:BLOCK, :] = dk_all[pl.ds(start, BLOCK), :].astype(bf16)
            ref[BLOCK:, :] = dv_all[pl.ds(start, BLOCK), :].astype(bf16)


def student_backward(meta, sel, queries, weights, grad_pieces, kv_blocks):
    rows = BLOCK // BS
    return pl.pallas_call(
        student_backward_kernel,
        grid=(rows,),
        in_specs=[
            pl.BlockSpec(memory_space=SMEM),
            pl.BlockSpec(memory_space=SMEM),
            pl.BlockSpec((BS, HD), lambda i: (i, 0)),
            pl.BlockSpec((BS, NSEL * BS), lambda i: (i, 0)),
            pl.BlockSpec((8, BS, HD), lambda i: (0, i, 0)),
        ]
        + [pl.BlockSpec(memory_space=pltpu.VMEM)] * 8,
        out_specs=[pl.BlockSpec((BS, HD), lambda i: (i, 0))] + [pl.BlockSpec(memory_space=pltpu.VMEM)] * 8,
        out_shape=[jax.ShapeDtypeStruct((BLOCK, HD), f32)]
        + [jax.ShapeDtypeStruct((2 * BLOCK, HD), bf16)] * 8,
        scratch_shapes=[pltpu.VMEM((8 * BLOCK, HD), bf16)] * 2
        + [pltpu.VMEM((8 * BLOCK, HD), f32)] * 2,
        compiler_params=pltpu.CompilerParams(vmem_limit_bytes=48 << 20),
        cost_estimate=pl.CostEstimate(
            flops=8 * BLOCK * NSEL * BS * HD, bytes_accessed=15 << 20, transcendentals=0
        ),
        name="student_backward",
    )(meta, sel, queries, weights, grad_pieces, *kv_blocks)


def project_kernel(transposed, added, where, s_ref, a_ref, b_ref, w_ref, *refs):
    acc = None
    for ref, j in ((s_ref, 0), (a_ref, 1 + where[1]), (b_ref, 2 - where[1])):
        span = pl.ds(pl.multiple_of(j * HD, HD), HD)
        if transposed:
            part = lax.dot_general(ref[...], w_ref[:, span], ROWS_NT, preferred_element_type=f32)
        else:
            part = jnp.dot(ref[...], w_ref[span, :], preferred_element_type=f32)
        acc = part if acc is None else acc + part
    if added:
        acc = acc + refs[0][0].astype(f32)
    refs[-1][0] = acc.astype(bf16)


def project(where, attn, weight, width, transposed, extra=None):
    def piece(p, at):
        return (p // 2) * 4 + at[0] * 2 + p % 2

    if transposed:
        w_spec = pl.BlockSpec((width, 3 * HD), lambda p, c: (piece(p, c), 0))
    else:
        w_spec = pl.BlockSpec((3 * HD, width), lambda p, c: (0, piece(p, c)))
    out_spec = pl.BlockSpec((1, BLOCK, width), lambda p, c: (p, 0, 0))
    args = list(attn) + [weight] + ([] if extra is None else [extra])

    def kernel(*refs):
        project_kernel(transposed, extra is not None, *refs)

    return pl.pallas_call(
        kernel,
        grid_spec=pltpu.PrefetchScalarGridSpec(
            num_scalar_prefetch=1,
            grid=(8,),
            in_specs=[pl.BlockSpec((BLOCK, HD), lambda p, c: (0, 0))] * 3
            + [w_spec]
            + ([] if extra is None else [out_spec]),
            out_specs=out_spec,
        ),
        out_shape=jax.ShapeDtypeStruct((8, BLOCK, width), bf16),
        compiler_params=pltpu.CompilerParams(vmem_limit_bytes=32 << 20),
        cost_estimate=pl.CostEstimate(
            flops=2 * 8 * BLOCK * width * 3 * HD,
            bytes_accessed=2 * 8 * BLOCK * width * (1 if extra is None else 2) + (2 << 20),
            transcendentals=0,
        ),
        name="project_grad" if transposed else "project_mismatch",
    )(where, *args)


def on_device(t_query, t_key, t_value, t_out, s_query, s_key, s_value, s_out, segments, selection):
    x, y, core = lax.axis_index("xlo"), lax.axis_index("y"), lax.axis_index("core")
    mine = 4 * x + y
    partner = 4 * (1 - x) + y

    def half(array, which, axis=1):
        return lax.dynamic_slice_in_dim(array, which * HD, HD, axis)

    def along_y(block, all_x, causal_x):
        return tuple(
            lax.ppermute(block, BLK, y_pairs(shift, all_x, causal_x)) for shift in (1, -1, 2)
        )

    to_partner = [(i, i ^ 4) for i in range(8)]
    spots = jnp.stack([y, (y + 3) % 4, (y + 1) % 4, (y + 2) % 4]).astype(jnp.int32)

    zeros = jnp.sum((segments == 0).reshape(8, HD).astype(f32), axis=0, keepdims=True)
    zeros = jnp.pad(zeros, ((0, 15), (0, 0))).astype(bf16)

    s_own = jnp.concatenate([s_key, s_value, zeros], axis=0)
    s_near = along_y(s_own, (0,), (1,))
    sent = jnp.concatenate([half(t_key, 1 - x), half(t_value, 1 - x), zeros], axis=0)
    t_got = lax.ppermute(sent, BLK, to_partner)
    q_got = lax.ppermute(half(t_query, 1 - x), BLK, to_partner)
    t_own = jnp.concatenate([half(t_key, x), half(t_value, x), zeros], axis=0)
    t_near = along_y(t_own, (0,), (1,))
    t_far = along_y(t_got, (1,), (0,))
    up = [(i, i + 4) for i in range(4)]
    s_low = tuple(lax.ppermute(block, BLK, up) for block in (s_own,) + s_near)

    weight = jnp.concatenate([s_out, -t_out], axis=0)
    rows = lax.dynamic_slice_in_dim(s_out, mine * (HD // 8), HD // 8, 0)
    rows = lax.all_gather(rows, GROUP, axis=0, tiled=True)
    rows, t_near = lax.optimization_barrier((rows, t_near))
    through = lax.dot_general(rows, weight, ROWS_NT, preferred_element_type=f32).astype(bf16)
    through = lax.all_gather(through, BLK, axis=0, tiled=True)
    through = through.reshape(8, 16, HD // 8, 3 * HD).transpose(1, 0, 2, 3).reshape(16 * HD, 3 * HD)

    def meta_of(first, order):
        head = jnp.stack([first] + [jnp.int32(0)] * 7).astype(jnp.int32)
        return jnp.concatenate([head, order, spots, 4 + spots])

    order = jnp.concatenate([4 * x + spots, 4 * (1 - x) + spots]).astype(jnp.int32)
    sel = selection.reshape(-1)
    k_pos = (selection[:, :, None] * BS + jnp.arange(BS, dtype=jnp.int32)).reshape(-1, 1, NSEL * BS)

    s_blocks = (s_own,) + s_near + s_low
    s_attn, weights = student_forward(meta_of(mine, order), sel, s_query, k_pos, s_blocks)

    t_blocks = (t_own,) + t_near + (t_got,) + t_far
    away = teacher_attention(meta_of(partner, order), q_got, t_blocks)
    back = lax.ppermute(away, BLK, to_partner)
    here = teacher_attention(meta_of(mine, order), half(t_query, x), t_blocks)

    attn = (s_attn, here, back)
    this = jnp.stack([core, x]).astype(jnp.int32)
    other = jnp.stack([1 - core, x]).astype(jnp.int32)
    to_core = [(0, 1), (1, 0)]
    grad = project(other, attn, through, HD, True)
    grad = lax.ppermute(grad, "core", to_core)
    grad = project(this, attn, through, HD, True, grad)
    attn, grad = lax.optimization_barrier((attn, grad))
    grad = lax.all_to_all(grad, ZX, 0, 0, tiled=True)

    part = project(other, attn, weight, 2 * HD, False)
    part = lax.ppermute(part, "core", to_core)
    part = project(this, attn, weight, 2 * HD, False, part)
    part, grad = lax.optimization_barrier((part, grad))
    part = lax.all_to_all(part, ZX, 0, 0, tiled=True)

    out = student_backward(meta_of(mine, order), sel, s_query, weights, grad, s_blocks)
    s_dq, pieces = out[0], out[1:]

    def earlier(shift, all_x, causal_x):
        pairs = []
        for i in range(2):
            for j in range(4):
                to = (j + shift) % 4
                if i in all_x or (i in causal_x and to < j):
                    pairs.append((4 * i + j, 4 * i + to))
        return pairs

    low, high = pieces[:4], pieces[4:]
    low_sum, high_sum = low[0].astype(f32), high[0].astype(f32)
    for j, shift in ((1, -1), (2, 1), (3, 2)):
        low_sum += lax.ppermute(low[j], BLK, earlier(shift, (1,), (0,))).astype(f32)
    for j, shift in ((1, -1), (2, 1), (3, 2)):
        high_sum += lax.ppermute(high[j], BLK, earlier(shift, (), (1,))).astype(f32)
    across = lax.ppermute(low_sum.astype(bf16), BLK, [(i + 4, i) for i in range(4)])
    total = jnp.where(x == 0, low_sum + across.astype(f32), high_sum)

    mismatch = jnp.sum(part.astype(f32), axis=0)
    return mismatch, s_dq, total[:BLOCK], total[BLOCK:]


def solution(mesh):
    fine = Mesh(mesh.devices.reshape(2, 4, 4, 2, 2), ("xlo", "y", "z", "core", "xhi"))
    data = P(BLK, GROUP)
    flat = P(GROUP, None)
    return jax.shard_map(
        on_device,
        mesh=fine,
        in_specs=(data, data, data, flat, data, data, data, flat, P(BLK), P(BLK, None)),
        out_specs=(data, data, data, data),
        check_vma=False,
    )
```

```python
import jax
import jax.numpy as jnp
from jax import lax
from jax.experimental import pallas as pl
from jax.experimental.pallas import tpu as pltpu
from jax.sharding import Mesh
from jax.sharding import PartitionSpec as P

HD = 128
BS = 64
NSEL = 16
BLOCK = 1024
COUNTS = 16
FORWARD_ROWS = 4
BACKWARD_ROWS = 4
TILE_Q = 512
TILE_K = 512
SCALE = HD ** (-0.5)
EXP_SCALE = SCALE * 1.4426950408889634
LOWEST = -1e30

BLK = ("xlo", "y")
GROUP = ("z", "core", "xhi")
ZX = ("z", "xhi")
f32 = jnp.float32
bf16 = jnp.bfloat16

SMEM = pltpu.SMEM
ANY = pl.BlockSpec(memory_space=pl.ANY)
FAR = pl.BlockSpec(memory_space=pltpu.HBM)

VMEM = pl.BlockSpec(memory_space=pltpu.VMEM)
ROWS_NT = (((1,), (1,)), ((), ()))
ROWS_TN = (((0,), (0,)), ((), ()))


def y_pairs(shift, all_x, causal_x):
    pairs = []
    for x in range(2):
        for y in range(4):
            to = (y + shift) % 4
            if x in all_x or (x in causal_x and y < to):
                pairs.append((4 * x + y, 4 * x + to))
    return pairs


def far(array):
    return pltpu.with_memory_space_constraint(array, pltpu.HBM)


SPAN = 2 * BLOCK + COUNTS


def blocks_of(refs):
    return [(ref, k * SPAN) for ref in refs for k in range(ref.shape[0] // SPAN)]


def load(blocks, key_all, value_all, counts, sems):
    copies = []

    def bring(source, target):
        copy = pltpu.make_async_copy(source, target, sems.at[len(copies)])
        copy.start()
        copies.append(copy)

    for j, (ref, at) in enumerate(blocks):
        slot = pl.ds(j * BLOCK, BLOCK)
        bring(ref.at[pl.ds(at, BLOCK)], key_all.at[slot])
        bring(ref.at[pl.ds(at + BLOCK, BLOCK)], value_all.at[slot])
        if counts is not None:
            bring(ref.at[pl.ds(at + 2 * BLOCK, COUNTS)], counts.at[pl.ds(j * COUNTS, COUNTS)])
    for copy in copies:
        copy.wait()


def border_of(counts):
    return jnp.sum(counts[...].astype(f32)).astype(jnp.int32)


KEYS = [pltpu.VMEM((8 * BLOCK, HD), bf16)] * 2
WITH_COUNTS = KEYS + [pltpu.VMEM((8 * COUNTS, HD), bf16), pltpu.SemaphoreType.DMA((24,))]


def teacher_kernel(meta, away_ref, here_ref, *refs):
    blocks = blocks_of(refs[:-6])
    away_out, here_out, key_all, value_all, counts, sems = refs[-6:]
    load(blocks, key_all, value_all, counts, sems)
    border = border_of(counts)
    per_block = BLOCK // TILE_K

    def one_tile(q_ref, o_ref, block, step):
        first = block * BLOCK + step * TILE_Q
        low_first = jnp.where(first >= border, border, 0)
        low_last = jnp.where(first + TILE_Q - 1 >= border, border, 0)
        span = pl.ds(step * TILE_Q, TILE_Q)
        queries = q_ref[span, :]
        q_pos = first + lax.broadcasted_iota(jnp.int32, (TILE_Q, 1), 0)
        q_low = jnp.where(q_pos >= border, border, 0)

        def turn(masked, j, carry):
            largest, total, acc = carry
            slot = meta[8 + j // per_block]
            start = pl.multiple_of(slot * BLOCK + (j % per_block) * TILE_K, TILE_K)
            scores = lax.dot_general(
                queries, key_all[pl.ds(start, TILE_K), :], ROWS_NT, preferred_element_type=f32
            )
            if masked:
                k_pos = j * TILE_K + lax.broadcasted_iota(jnp.int32, (1, TILE_K), 1)
                scores = jnp.where((k_pos <= q_pos) & (k_pos >= q_low), scores, LOWEST)
            new = jnp.maximum(largest, jnp.max(scores, axis=1, keepdims=True))
            factor = jnp.exp2((largest - new) * EXP_SCALE)
            weights = jnp.exp2((scores - new) * EXP_SCALE)
            total = factor * total + jnp.sum(weights, axis=1, keepdims=True)
            acc = factor * acc + jnp.dot(
                weights.astype(bf16), value_all[pl.ds(start, TILE_K), :], preferred_element_type=f32
            )
            return new, total, acc

        carry = (
            jnp.full((TILE_Q, 1), LOWEST, f32),
            jnp.zeros((TILE_Q, 1), f32),
            jnp.zeros((TILE_Q, HD), f32),
        )
        begin = low_first // TILE_K
        diagonal = first // TILE_K
        clear = jnp.minimum((low_last + TILE_K - 1) // TILE_K, diagonal)
        carry = lax.fori_loop(begin, clear, lambda j, c: turn(True, j, c), carry)
        carry = lax.fori_loop(clear, diagonal, lambda j, c: turn(False, j, c), carry)
        for j in range(max(TILE_Q // TILE_K, 1)):
            carry = turn(True, diagonal + j, carry)
        _, total, acc = carry
        o_ref[span, :] = (acc / total).astype(bf16)

    for step in range(BLOCK // TILE_Q):
        one_tile(away_ref, away_out, meta[1], step)
    for step in range(BLOCK // TILE_Q):
        one_tile(here_ref, here_out, meta[0], step)


def teacher_attention(meta, away, here, kv_blocks):
    return pl.pallas_call(
        teacher_kernel,
        in_specs=[pl.BlockSpec(memory_space=SMEM), VMEM, VMEM] + [FAR] * len(kv_blocks),
        out_specs=[pl.BlockSpec((BLOCK, HD), lambda: (0, 0))] * 2,
        out_shape=[pltpu.HBM((BLOCK, HD), bf16)] * 2,
        scratch_shapes=WITH_COUNTS,
        compiler_params=pltpu.CompilerParams(vmem_limit_bytes=24 << 20),
        cost_estimate=pl.CostEstimate(
            flops=8 * 4 * BLOCK * BLOCK * HD, bytes_accessed=5 << 20, transcendentals=8 * BLOCK * BLOCK
        ),
        name="teacher_attention",
    )(meta, away, here, *map(far, kv_blocks))


def chosen_rows(sel, row, table):
    pieces = []
    for n in range(NSEL):
        start = pl.multiple_of(sel[row * NSEL + n], BS)
        pieces.append(table[pl.ds(start, BS), :])
    return jnp.concatenate(pieces, axis=0)


def student_forward_kernel(meta, sel, q_ref, kpos_ref, *refs):
    blocks = blocks_of(refs[:-6])
    o_ref, p_ref, key_all, value_all, counts, sems = refs[-6:]
    step = pl.program_id(0)

    @pl.when(step == 0)
    def _():
        load(blocks, key_all, value_all, counts, sems)

    border = border_of(counts)
    for u in range(FORWARD_ROWS):
        row = step * FORWARD_ROWS + u
        span = pl.ds(u * BS, BS)
        q_pos = meta[0] * BLOCK + row * BS + lax.broadcasted_iota(jnp.int32, (BS, 1), 0)
        q_low = jnp.where(q_pos >= border, border, 0)
        k_pos = kpos_ref[u]
        scores = lax.dot_general(
            q_ref[span, :], chosen_rows(sel, row, key_all), ROWS_NT, preferred_element_type=f32
        )
        scores = jnp.where((k_pos <= q_pos) & (k_pos >= q_low), scores, LOWEST)
        weights = jnp.exp2((scores - jnp.max(scores, axis=1, keepdims=True)) * EXP_SCALE)
        inverse = 1.0 / jnp.sum(weights, axis=1, keepdims=True)
        p_ref[span, :] = weights * inverse
        blended = jnp.dot(
            weights.astype(bf16), chosen_rows(sel, row, value_all), preferred_element_type=f32
        )
        o_ref[span, :] = (blended * inverse).astype(bf16)


def student_forward(meta, sel, queries, k_pos, kv_blocks):
    size = FORWARD_ROWS * BS
    return pl.pallas_call(
        student_forward_kernel,
        grid=(BLOCK // size,),
        in_specs=[
            pl.BlockSpec(memory_space=SMEM),
            pl.BlockSpec(memory_space=SMEM),
            pl.BlockSpec((size, HD), lambda i: (i, 0)),
            pl.BlockSpec((FORWARD_ROWS, 1, NSEL * BS), lambda i: (i, 0, 0)),
        ]
        + [FAR] * len(kv_blocks),
        out_specs=[
            pl.BlockSpec((size, HD), lambda i: (i, 0)),
            pl.BlockSpec((size, NSEL * BS), lambda i: (i, 0)),
        ],
        out_shape=[
            pltpu.HBM((BLOCK, HD), bf16),
            pltpu.HBM((BLOCK, NSEL * BS), f32),
        ],
        scratch_shapes=WITH_COUNTS,
        compiler_params=pltpu.CompilerParams(vmem_limit_bytes=24 << 20),
        cost_estimate=pl.CostEstimate(
            flops=4 * BLOCK * NSEL * BS * HD, bytes_accessed=9 << 20, transcendentals=BLOCK * NSEL * BS
        ),
        name="student_forward",
    )(meta, sel, queries, k_pos, *map(far, kv_blocks))


def student_backward_kernel(meta, sel, q_ref, p_ref, g_ref, *refs):
    blocks = blocks_of(refs[:-14])
    dq_ref, out_refs = refs[-14], refs[-13:-5]
    key_all, value_all, sems, dk_all, dv_all = refs[-5:]
    step = pl.program_id(0)

    @pl.when(step == 0)
    def _():
        load(blocks, key_all, value_all, None, sems)
        dk_all[...] = jnp.zeros_like(dk_all)
        dv_all[...] = jnp.zeros_like(dv_all)

    for u in range(BACKWARD_ROWS):
        row = step * BACKWARD_ROWS + u
        span = pl.ds(u * BS, BS)
        grad = jnp.sum(g_ref[:, span, :].astype(f32), axis=0).astype(bf16)
        weights = p_ref[span, :]
        weight_grad = lax.dot_general(
            grad, chosen_rows(sel, row, value_all), ROWS_NT, preferred_element_type=f32
        )
        row_dots = jnp.sum(weights * weight_grad, axis=1, keepdims=True)
        score_grad = (weights * (weight_grad - row_dots) * SCALE).astype(bf16)
        dq_ref[span, :] = jnp.dot(
            score_grad, chosen_rows(sel, row, key_all), preferred_element_type=f32
        )
        key_grad = lax.dot_general(score_grad, q_ref[span, :], ROWS_TN, preferred_element_type=f32)
        value_grad = lax.dot_general(
            weights.astype(bf16), grad, ROWS_TN, preferred_element_type=f32
        )
        for n in range(NSEL):
            start = pl.multiple_of(sel[row * NSEL + n], BS)
            dk_all[pl.ds(start, BS), :] += key_grad[n * BS : (n + 1) * BS, :]
            dv_all[pl.ds(start, BS), :] += value_grad[n * BS : (n + 1) * BS, :]

    @pl.when(step == pl.num_programs(0) - 1)
    def _():
        copies = []
        for j in (4, 5, 6, 7, 0, 1, 2, 3):
            ref = out_refs[j]
            start = pl.multiple_of((meta[1] * 4 + j) % 8 * BLOCK, BLOCK)
            for k, (total, table) in enumerate(((dk_all, key_all), (dv_all, value_all))):
                spot = pl.ds(k * BLOCK, BLOCK)
                if j < 4:
                    ref[spot, :] = total[pl.ds(start, BLOCK), :].astype(bf16)
                    continue
                slot = pl.ds((j - 4) * BLOCK, BLOCK)
                table[slot, :] = total[pl.ds(start, BLOCK), :].astype(bf16)
                copy = pltpu.make_async_copy(table.at[slot], ref.at[spot], sems.at[len(copies)])
                copy.start()
                copies.append(copy)
        for copy in copies:
            copy.wait()


def student_backward(meta, sel, queries, weights, grad_pieces, kv_blocks):
    size = BACKWARD_ROWS * BS
    return pl.pallas_call(
        student_backward_kernel,
        grid=(BLOCK // size,),
        in_specs=[
            pl.BlockSpec(memory_space=SMEM),
            pl.BlockSpec(memory_space=SMEM),
            pl.BlockSpec((size, HD), lambda i: (i, 0)),
            pl.BlockSpec((size, NSEL * BS), lambda i: (i, 0)),
            pl.BlockSpec((8, size, HD), lambda i: (0, i, 0)),
        ]
        + [FAR] * len(kv_blocks),
        out_specs=[pl.BlockSpec((size, HD), lambda i: (i, 0))] + [VMEM] * 4 + [FAR] * 4,
        out_shape=[jax.ShapeDtypeStruct((BLOCK, HD), f32)]
        + [jax.ShapeDtypeStruct((2 * BLOCK, HD), bf16)] * 4
        + [pltpu.HBM((2 * BLOCK, HD), bf16)] * 4,
        scratch_shapes=KEYS + [pltpu.SemaphoreType.DMA((16,))] + [pltpu.VMEM((8 * BLOCK, HD), f32)] * 2,
        compiler_params=pltpu.CompilerParams(vmem_limit_bytes=32 << 20),
        cost_estimate=pl.CostEstimate(
            flops=8 * BLOCK * NSEL * BS * HD, bytes_accessed=15 << 20, transcendentals=0
        ),
        name="student_backward",
    )(meta, sel, queries, far(weights), grad_pieces, *map(far, kv_blocks))


def project(where, attn, weights, width, extra=None, after=()):
    composed = len(weights) == 1

    def piece(p, at):
        return (p // 2) * 4 + at[0] * 2 + p % 2

    if composed:
        w_specs = [pl.BlockSpec((8, 1, COUNTS, 3 * HD), lambda p, c: (0, piece(p, c), 0, 0))]
    else:
        w_specs = [
            pl.BlockSpec((HD, width), lambda p, c: (0, piece(p, c))),
            pl.BlockSpec((2 * HD, width), lambda p, c: (0, piece(p, c))),
        ]
    out_spec = pl.BlockSpec((1, BLOCK, width), lambda p, c: (p, 0, 0))
    more = [] if extra is None else [extra]
    args = list(attn) + list(weights) + more + list(after)

    def kernel(at, s_ref, a_ref, b_ref, *refs):
        near = pl.multiple_of(at[1] * HD, HD)
        far = pl.multiple_of((1 - at[1]) * HD, HD)
        if composed:
            wide = refs[0][...].reshape(HD, 3 * HD)
            here, back = a_ref[...], b_ref[...]
            first = jnp.where(at[1] == 0, here, back)
            second = jnp.where(at[1] == 0, back, here)

            def times(value, j):
                return lax.dot_general(
                    value, wide[:, j * HD : (j + 1) * HD], ROWS_NT, preferred_element_type=f32
                )

            acc = times(s_ref[...], 0) - times(first, 1) - times(second, 2)
        else:
            acc = jnp.dot(s_ref[...], refs[0][...], preferred_element_type=f32)
            acc -= jnp.dot(a_ref[...], refs[1][pl.ds(near, HD), :], preferred_element_type=f32)
            acc -= jnp.dot(b_ref[...], refs[1][pl.ds(far, HD), :], preferred_element_type=f32)
        if extra is not None:
            acc = acc + refs[len(weights)][0].astype(f32)
        refs[-1][0] = acc.astype(bf16)

    return pl.pallas_call(
        kernel,
        grid_spec=pltpu.PrefetchScalarGridSpec(
            num_scalar_prefetch=1,
            grid=(8,),
            in_specs=[pl.BlockSpec((BLOCK, HD), lambda p, c: (0, 0))] * 3
            + w_specs
            + [out_spec] * len(more)
            + [ANY] * len(after),
            out_specs=out_spec,
        ),
        out_shape=(pltpu.HBM if more else jax.ShapeDtypeStruct)((8, BLOCK, width), bf16),
        compiler_params=pltpu.CompilerParams(vmem_limit_bytes=16 << 20),
        cost_estimate=pl.CostEstimate(
            flops=2 * 8 * BLOCK * width * 3 * HD,
            bytes_accessed=2 * 8 * BLOCK * width * (1 + len(more)) + (2 << 20),
            transcendentals=0,
        ),
        name="project_grad" if composed else "project_mismatch",
    )(where, *args)


def token(*arrays):
    total = None
    for array in arrays:
        corner = array[:COUNTS, :] if array.ndim == 2 else array[0, :COUNTS, :]
        total = corner if total is None else total + corner
    return total


def gate(values, after):
    def kernel(*refs):
        pass

    n = len(values)
    return tuple(
        pl.pallas_call(
            kernel,
            in_specs=[FAR] * n + [ANY] * len(after),
            out_specs=[FAR] * n,
            out_shape=[pltpu.HBM(v.shape, v.dtype) for v in values],
            input_output_aliases={k: k for k in range(n)},
            name="gate",
        )(*map(far, values), *after)
    )


def pack_kernel(at, seg_ref, tq_ref, tk_ref, tv_ref, sk_ref, sv_ref, so_ref, *refs):
    outs, stages, sems = refs[:6], refs[6:12], refs[12]
    s_own, t_own, t_sent, q_own, q_sent, rows = stages
    near = pl.ds(pl.multiple_of(at[0] * HD, HD), HD)
    other = pl.ds(pl.multiple_of((1 - at[0]) * HD, HD), HD)
    started = 0

    def move(source, target):
        nonlocal started
        copy = pltpu.make_async_copy(source, target, sems.at[started])
        copy.start()
        started += 1
        return copy

    keys, values, last = pl.ds(0, BLOCK), pl.ds(BLOCK, BLOCK), pl.ds(2 * BLOCK, COUNTS)
    part = pl.ds(pl.multiple_of(at[1] * COUNTS, COUNTS), COUNTS)
    coming = (
        (0, [move(sk_ref, s_own.at[keys]), move(sv_ref, s_own.at[values])]),
        (2, [move(tk_ref.at[:, other], t_sent.at[keys]), move(tv_ref.at[:, other], t_sent.at[values])]),
        (4, [move(tq_ref.at[:, other], q_sent)]),
        (5, [move(so_ref.at[part], rows)]),
        (1, [move(tk_ref.at[:, near], t_own.at[keys]), move(tv_ref.at[:, near], t_own.at[values])]),
        (3, [move(tq_ref.at[:, near], q_own)]),
    )
    found = jnp.sum((seg_ref[...] == 0).astype(f32), axis=0, keepdims=True)
    first = lax.broadcasted_iota(jnp.int32, (COUNTS, HD), 0) == 0
    counts = jnp.where(first, found, 0.0).astype(bf16)
    for stage in (s_own, t_own, t_sent):
        stage[last, :] = counts
    going = []
    for k, copies in coming:
        for copy in copies:
            copy.wait()
        going.append(move(stages[k], outs[k]))
    for copy in going:
        copy.wait()


def pack(at, seg, *arrays):
    shapes = [(SPAN, HD)] * 3 + [(BLOCK, HD)] * 2 + [(COUNTS, arrays[-1].shape[1])]
    return pl.pallas_call(
        pack_kernel,
        in_specs=[pl.BlockSpec(memory_space=SMEM), VMEM] + [FAR] * 6,
        out_specs=[FAR] * 6,
        out_shape=[pltpu.HBM(shape, bf16) for shape in shapes],
        scratch_shapes=[pltpu.VMEM(shape, bf16) for shape in shapes] + [pltpu.SemaphoreType.DMA((15,))],
        compiler_params=pltpu.CompilerParams(vmem_limit_bytes=8 << 20),
        cost_estimate=pl.CostEstimate(flops=0, bytes_accessed=5 << 20, transcendentals=0),
        name="pack",
    )(at, seg, *map(far, arrays))


def repack_kernel(*refs):
    for n, ref in enumerate(refs[:5]):
        target, k = (refs[-2], n) if n < 2 else (refs[-1], n - 2)
        target[k * SPAN : (k + 1) * SPAN, :] = ref[...]


def repack(teacher, student, after):
    return pl.pallas_call(
        repack_kernel,
        in_specs=[VMEM] * 5 + [ANY] * len(after),
        out_specs=[VMEM] * 2,
        out_shape=[jax.ShapeDtypeStruct((k * SPAN, HD), bf16) for k in (2, 3)],
        compiler_params=pltpu.CompilerParams(vmem_limit_bytes=8 << 20),
        cost_estimate=pl.CostEstimate(flops=0, bytes_accessed=5 << 20, transcendentals=0),
        name="repack",
    )(*teacher, *student, *after)


def compose_kernel(rows_ref, s_ref, t_ref, *refs):
    rows = rows_ref[...]
    for ref, low, high in ((s_ref, 0, HD), (t_ref, HD, 3 * HD)):
        refs[-1][:, low:high] = lax.dot_general(
            rows, ref[...], ROWS_NT, preferred_element_type=f32
        ).astype(bf16)


def compose(rows, s_out, t_out, after):
    return pl.pallas_call(
        compose_kernel,
        in_specs=[VMEM] * 3 + [ANY] * len(after),
        out_specs=VMEM,
        out_shape=jax.ShapeDtypeStruct((rows.shape[0], 3 * HD), bf16),
        compiler_params=pltpu.CompilerParams(vmem_limit_bytes=24 << 20),
        cost_estimate=pl.CostEstimate(
            flops=2 * rows.shape[0] * 3 * HD * rows.shape[1], bytes_accessed=5 << 20, transcendentals=0
        ),
        name="compose",
    )(rows, s_out, t_out, *after)


def add_pieces_kernel(in_ref, out_ref):
    out_ref[...] = jnp.sum(in_ref[...].astype(f32), axis=0)


def add_pieces(pieces):
    count, rows, width = pieces.shape
    size = rows // 4
    return pl.pallas_call(
        add_pieces_kernel,
        grid=(4,),
        in_specs=[pl.BlockSpec((count, size, width), lambda i: (0, i, 0))],
        out_specs=pl.BlockSpec((size, width), lambda i: (i, 0)),
        out_shape=jax.ShapeDtypeStruct((rows, width), f32),
        compiler_params=pltpu.CompilerParams(vmem_limit_bytes=16 << 20),
        cost_estimate=pl.CostEstimate(flops=8 << 20, bytes_accessed=5 << 20, transcendentals=0),
        name="add_pieces",
    )(pieces)


def finish_kernel(at, *refs):
    low, across, high, (dk_ref, dv_ref) = refs[:4], refs[4], refs[5:9], refs[-2:]

    def write(parts):
        for ref, span in ((dk_ref, pl.ds(0, BLOCK)), (dv_ref, pl.ds(BLOCK, BLOCK))):
            total = parts[0][span, :].astype(f32)
            for part in parts[1:]:
                total = total + part[span, :].astype(f32)
            ref[...] = total

    @pl.when(at[0] == 0)
    def _():
        write(low + (across,))

    @pl.when(at[0] == 1)
    def _():
        write(high)


def finish(at, low, across, high, after):
    near = [pltpu.with_memory_space_constraint(part, pltpu.VMEM) for part in (*low, across, *high)]
    return pl.pallas_call(
        finish_kernel,
        in_specs=[pl.BlockSpec(memory_space=SMEM)] + [VMEM] * 9 + [ANY] * len(after),
        out_specs=[pl.BlockSpec((BLOCK, HD), lambda: (0, 0))] * 2,
        out_shape=[pltpu.HBM((BLOCK, HD), f32)] * 2,
        compiler_params=pltpu.CompilerParams(vmem_limit_bytes=16 << 20),
        cost_estimate=pl.CostEstimate(flops=4 << 20, bytes_accessed=5 << 20, transcendentals=0),
        name="finish",
    )(at, *near, *after)


def on_device(t_query, t_key, t_value, t_out, s_query, s_key, s_value, s_out, segments, selection):
    x, y, core = lax.axis_index("xlo"), lax.axis_index("y"), lax.axis_index("core")
    mine = 4 * x + y
    partner = 4 * (1 - x) + y

    def along_y(block, all_x, causal_x):
        return tuple(
            lax.ppermute(block, BLK, y_pairs(shift, all_x, causal_x)) for shift in (1, -1, 2)
        )

    to_partner = [(i, i ^ 4) for i in range(8)]
    at_x = jnp.stack([x, mine]).astype(jnp.int32)
    s_own, t_own, t_sent, q_own, q_sent, rows = pack(
        at_x, segments.reshape(8, HD), t_query, t_key, t_value, s_key, s_value, s_out
    )
    up = [(i, i + 4) for i in range(4)]
    s_near = along_y(s_own, (0,), (1,))
    t_got = lax.ppermute(t_sent, BLK, to_partner)
    s_low = lax.ppermute(s_own, BLK, up)
    t_two, s_three = repack((t_own, t_got), s_near, (token(s_low),))
    t_near = along_y(t_two, (0, 1), ())
    s_lows = lax.ppermute(s_three, BLK, up)
    q_got = lax.ppermute(q_sent, BLK, to_partner)

    rows = lax.all_gather(rows, GROUP, axis=0, tiled=True)
    through = compose(rows, s_out, t_out, (token(*t_near, s_lows, q_got),))
    through = lax.all_gather(through, BLK, axis=0, tiled=True).reshape(8, 16, HD // 8, 3 * HD)

    def place_of(block):
        step = (block + 4 - y) % 4
        return jnp.where(step == 0, 0, jnp.where(step == 3, 1, step + 1)), (block // 4 != x).astype(jnp.int32)

    near, half = place_of(jnp.arange(8, dtype=jnp.int32))
    t_meta = jnp.concatenate([jnp.stack([mine, partner] + [0] * 6).astype(jnp.int32), 2 * near + half])
    near, half = place_of(selection // 16)
    sel = ((near + 4 * half) * BLOCK + selection % 16 * BS).reshape(-1).astype(jnp.int32)
    k_pos = (selection[:, :, None] * BS + jnp.arange(BS, dtype=jnp.int32)).reshape(-1, 1, NSEL * BS)
    s_meta = jnp.stack([mine, x]).astype(jnp.int32)

    t_blocks = (t_own, t_got, *t_near)
    away, here = teacher_attention(t_meta, q_got, q_own, t_blocks)
    back = lax.ppermute(away, BLK, to_partner)
    s_blocks = (s_own, *s_near, s_low, s_lows)
    s_attn, weights = student_forward(s_meta, sel, s_query, k_pos, s_blocks)
    attn = (s_attn, here, back)

    this = jnp.stack([core, x]).astype(jnp.int32)
    other = jnp.stack([1 - core, x]).astype(jnp.int32)
    to_core = [(0, 1), (1, 0)]
    grad = project(other, attn, (through,), HD)
    grad = lax.ppermute(grad, "core", to_core)
    grad = project(this, attn, (through,), HD, grad)
    part = project(other, attn, (s_out, t_out), 2 * HD, None, (token(grad),))
    grad = lax.all_to_all(grad, ZX, 0, 0, tiled=True)
    part = lax.ppermute(part, "core", to_core)
    part = project(this, attn, (s_out, t_out), 2 * HD, part)
    part = lax.all_to_all(part, ZX, 0, 0, tiled=True)

    out = student_backward(s_meta, sel, s_query, weights, grad, s_blocks)
    s_dq, pieces = out[0], out[1:]

    def earlier(shift, all_x, causal_x):
        pairs = []
        for i in range(2):
            for j in range(4):
                to = (j + shift) % 4
                if i in all_x or (i in causal_x and to < j):
                    pairs.append((4 * i + j, 4 * i + to))
        return pairs

    low, high = list(pieces[:4]), list(pieces[4:])
    for j, shift in ((1, -1), (2, 1), (3, 2)):
        low[j] = lax.ppermute(low[j], BLK, earlier(shift, (1,), (0,)))
    low_sum = low[0].astype(f32) + low[1].astype(f32) + low[2].astype(f32) + low[3].astype(f32)
    across = low_sum.astype(bf16)
    high = list(gate(high, (token(across),)))
    across = lax.ppermute(across, BLK, [(i + 4, i) for i in range(4)])
    for j, shift in ((1, -1), (2, 1), (3, 2)):
        high[j] = lax.ppermute(high[j], BLK, earlier(shift, (), (1,)))
    mismatch = add_pieces(part)
    s_dk, s_dv = finish(at_x, tuple(low), across, tuple(high), (token(mismatch[:, :HD]),))
    return mismatch, s_dq, s_dk, s_dv


def solution(mesh):
    fine = Mesh(mesh.devices.reshape(2, 4, 4, 2, 2), ("xlo", "y", "z", "core", "xhi"))
    data = P(BLK, GROUP)
    flat = P(GROUP, None)
    return jax.shard_map(
        on_device,
        mesh=fine,
        in_specs=(data, data, data, flat, data, data, data, flat, P(BLK), P(BLK, None)),
        out_specs=(data, data, data, data),
        check_vma=False,
    )
```

```python
import jax
import jax.numpy as jnp
from jax import lax
from jax.experimental import pallas as pl
from jax.experimental.pallas import tpu as pltpu
from jax.sharding import Mesh
from jax.sharding import PartitionSpec as P

HD = 128
BS = 64
NSEL = 16
BLOCK = 1024
COUNTS = 16
FORWARD_ROWS = 4
BACKWARD_ROWS = 4
TILE_Q = 512
TILE_K = 512
SCALE = HD ** (-0.5)
EXP_SCALE = SCALE * 1.4426950408889634
LOWEST = -1e30

BLK = ("xlo", "y")
GROUP = ("z", "core", "xhi")
ZX = ("z", "xhi")
f32 = jnp.float32
bf16 = jnp.bfloat16

SMEM = pltpu.SMEM
ANY = pl.BlockSpec(memory_space=pl.ANY)
FAR = pl.BlockSpec(memory_space=pltpu.HBM)

VMEM = pl.BlockSpec(memory_space=pltpu.VMEM)
ROWS_NT = (((1,), (1,)), ((), ()))
ROWS_TN = (((0,), (0,)), ((), ()))


def y_pairs(shift, all_x, causal_x):
    pairs = []
    for x in range(2):
        for y in range(4):
            to = (y + shift) % 4
            if x in all_x or (x in causal_x and y < to):
                pairs.append((4 * x + y, 4 * x + to))
    return pairs


def far(array):
    return pltpu.with_memory_space_constraint(array, pltpu.HBM)


SPAN = 2 * BLOCK + COUNTS


def blocks_of(refs):
    return [(ref, k * SPAN) for ref in refs for k in range(ref.shape[0] // SPAN)]


def load(blocks, key_all, value_all, counts, sems, meanwhile=None):
    copies = []

    def bring(source, target):
        copy = pltpu.make_async_copy(source, target, sems.at[len(copies)])
        copy.start()
        copies.append(copy)

    for j, (ref, at) in enumerate(blocks):
        slot = pl.ds(j * BLOCK, BLOCK)
        bring(ref.at[pl.ds(at, BLOCK)], key_all.at[slot])
        bring(ref.at[pl.ds(at + BLOCK, BLOCK)], value_all.at[slot])
        if counts is not None:
            bring(ref.at[pl.ds(at + 2 * BLOCK, COUNTS)], counts.at[pl.ds(j * COUNTS, COUNTS)])
    if meanwhile is not None:
        meanwhile()
    for copy in copies:
        copy.wait()


def border_of(counts):
    return jnp.sum(counts[...].astype(f32)).astype(jnp.int32)


KEYS = [pltpu.VMEM((8 * BLOCK, HD), bf16)] * 2
WITH_COUNTS = KEYS + [pltpu.VMEM((8 * COUNTS, HD), bf16), pltpu.SemaphoreType.DMA((24,))]


def teacher_kernel(meta, away_ref, here_ref, *refs):
    blocks = blocks_of(refs[:-6])
    away_out, here_out, key_all, value_all, counts, sems = refs[-6:]
    load(blocks, key_all, value_all, counts, sems)
    border = border_of(counts)
    per_block = BLOCK // TILE_K

    def one_block(q_ref, o_ref, block):
        first = block * BLOCK
        tiles = []
        for step in range(BLOCK // TILE_Q):
            q_pos = first + step * TILE_Q + lax.broadcasted_iota(jnp.int32, (TILE_Q, 1), 0)
            q_low = jnp.where(q_pos >= border, border, 0)
            tiles.append((q_ref[pl.ds(step * TILE_Q, TILE_Q), :], q_pos, q_low))

        def turn(masked, j, tile, carry):
            queries, q_pos, q_low = tile
            largest, total, acc = carry
            slot = meta[8 + j // per_block]
            start = pl.multiple_of(slot * BLOCK + (j % per_block) * TILE_K, TILE_K)
            scores = lax.dot_general(
                queries, key_all[pl.ds(start, TILE_K), :], ROWS_NT, preferred_element_type=f32
            )
            if masked:
                k_pos = j * TILE_K + lax.broadcasted_iota(jnp.int32, (1, TILE_K), 1)
                scores = jnp.where((k_pos <= q_pos) & (k_pos >= q_low), scores, LOWEST)
            new = jnp.maximum(largest, jnp.max(scores, axis=1, keepdims=True))
            factor = jnp.exp2((largest - new) * EXP_SCALE)
            weights = jnp.exp2((scores - new) * EXP_SCALE)
            total = factor * total + jnp.sum(weights, axis=1, keepdims=True)
            acc = factor * acc + jnp.dot(
                weights.astype(bf16), value_all[pl.ds(start, TILE_K), :], preferred_element_type=f32
            )
            return new, total, acc

        def turns(masked, j, carries):
            return tuple(turn(masked, j, tile, carry) for tile, carry in zip(tiles, carries))

        carries = tuple(
            (
                jnp.full((TILE_Q, 1), LOWEST, f32),
                jnp.zeros((TILE_Q, 1), f32),
                jnp.zeros((TILE_Q, HD), f32),
            )
            for _ in tiles
        )
        begin = jnp.where(first >= border, border, 0) // TILE_K
        diagonal = first // TILE_K
        low_last = jnp.where(first + BLOCK - 1 >= border, border, 0)
        clear = jnp.minimum((low_last + TILE_K - 1) // TILE_K, diagonal)
        carries = lax.fori_loop(begin, clear, lambda j, c: turns(True, j, c), carries)
        carries = lax.fori_loop(clear, diagonal, lambda j, c: turns(False, j, c), carries)
        carries = list(carries)
        for k in range(per_block):
            for n, tile in enumerate(tiles):
                if k * TILE_K < (n + 1) * TILE_Q:
                    carries[n] = turn(True, diagonal + k, tile, carries[n])
        for step, (_, total, acc) in enumerate(carries):
            o_ref[pl.ds(step * TILE_Q, TILE_Q), :] = (acc / total).astype(bf16)

    one_block(away_ref, away_out, meta[1])
    one_block(here_ref, here_out, meta[0])


def teacher_attention(meta, away, here, kv_blocks):
    return pl.pallas_call(
        teacher_kernel,
        in_specs=[pl.BlockSpec(memory_space=SMEM), VMEM, VMEM] + [ANY] * len(kv_blocks),
        out_specs=[pl.BlockSpec((BLOCK, HD), lambda: (0, 0))] * 2,
        out_shape=[pltpu.HBM((BLOCK, HD), bf16)] * 2,
        scratch_shapes=WITH_COUNTS,
        compiler_params=pltpu.CompilerParams(vmem_limit_bytes=24 << 20),
        cost_estimate=pl.CostEstimate(
            flops=8 * 4 * BLOCK * BLOCK * HD, bytes_accessed=5 << 20, transcendentals=8 * BLOCK * BLOCK
        ),
        name="teacher_attention",
    )(meta, away, here, *kv_blocks)


def chosen_rows(sel, row, table):
    pieces = []
    for n in range(NSEL):
        start = pl.multiple_of(sel[row * NSEL + n], BS)
        pieces.append(table[pl.ds(start, BS), :])
    return jnp.concatenate(pieces, axis=0)


def student_forward_kernel(meta, sel, q_ref, kpos_ref, *refs):
    blocks = blocks_of(refs[:-6])
    o_ref, p_ref, key_all, value_all, counts, sems = refs[-6:]
    step = pl.program_id(0)

    @pl.when(step == 0)
    def _():
        load(blocks, key_all, value_all, counts, sems)

    border = border_of(counts)
    for u in range(FORWARD_ROWS):
        row = step * FORWARD_ROWS + u
        span = pl.ds(u * BS, BS)
        q_pos = meta[0] * BLOCK + row * BS + lax.broadcasted_iota(jnp.int32, (BS, 1), 0)
        q_low = jnp.where(q_pos >= border, border, 0)
        k_pos = kpos_ref[u]
        scores = lax.dot_general(
            q_ref[span, :], chosen_rows(sel, row, key_all), ROWS_NT, preferred_element_type=f32
        )
        scores = jnp.where((k_pos <= q_pos) & (k_pos >= q_low), scores, LOWEST)
        weights = jnp.exp2((scores - jnp.max(scores, axis=1, keepdims=True)) * EXP_SCALE)
        inverse = 1.0 / jnp.sum(weights, axis=1, keepdims=True)
        p_ref[span, :] = weights * inverse
        blended = jnp.dot(
            weights.astype(bf16), chosen_rows(sel, row, value_all), preferred_element_type=f32
        )
        o_ref[span, :] = (blended * inverse).astype(bf16)


def student_forward(meta, sel, queries, k_pos, kv_blocks):
    size = FORWARD_ROWS * BS
    return pl.pallas_call(
        student_forward_kernel,
        grid=(BLOCK // size,),
        in_specs=[
            pl.BlockSpec(memory_space=SMEM),
            pl.BlockSpec(memory_space=SMEM),
            pl.BlockSpec((size, HD), lambda i: (i, 0)),
            pl.BlockSpec((FORWARD_ROWS, 1, NSEL * BS), lambda i: (i, 0, 0)),
        ]
        + [ANY] * len(kv_blocks),
        out_specs=[
            pl.BlockSpec((size, HD), lambda i: (i, 0)),
            pl.BlockSpec((size, NSEL * BS), lambda i: (i, 0)),
        ],
        out_shape=[
            pltpu.HBM((BLOCK, HD), bf16),
            pltpu.HBM((BLOCK, NSEL * BS), f32),
        ],
        scratch_shapes=WITH_COUNTS,
        compiler_params=pltpu.CompilerParams(vmem_limit_bytes=24 << 20),
        cost_estimate=pl.CostEstimate(
            flops=4 * BLOCK * NSEL * BS * HD, bytes_accessed=9 << 20, transcendentals=BLOCK * NSEL * BS
        ),
        name="student_forward",
    )(meta, sel, queries, k_pos, *kv_blocks)


def student_backward_kernel(meta, sel, q_ref, p_ref, g_ref, *refs):
    blocks = blocks_of(refs[:-14])
    dq_ref, out_refs = refs[-14], refs[-13:-5]
    key_all, value_all, sems, dk_all, dv_all = refs[-5:]
    step = pl.program_id(0)

    @pl.when(step == 0)
    def _():
        def clear():
            dk_all[...] = jnp.zeros_like(dk_all)
            dv_all[...] = jnp.zeros_like(dv_all)

        load(blocks, key_all, value_all, None, sems, clear)

    for u in range(BACKWARD_ROWS):
        row = step * BACKWARD_ROWS + u
        span = pl.ds(u * BS, BS)
        grad = jnp.sum(g_ref[:, span, :].astype(f32), axis=0).astype(bf16)
        weights = p_ref[span, :]
        weight_grad = lax.dot_general(
            grad, chosen_rows(sel, row, value_all), ROWS_NT, preferred_element_type=f32
        )
        row_dots = jnp.sum(weights * weight_grad, axis=1, keepdims=True)
        score_grad = (weights * (weight_grad - row_dots) * SCALE).astype(bf16)
        dq_ref[span, :] = jnp.dot(
            score_grad, chosen_rows(sel, row, key_all), preferred_element_type=f32
        )
        key_grad = lax.dot_general(score_grad, q_ref[span, :], ROWS_TN, preferred_element_type=f32)
        value_grad = lax.dot_general(
            weights.astype(bf16), grad, ROWS_TN, preferred_element_type=f32
        )
        for n in range(NSEL):
            start = pl.multiple_of(sel[row * NSEL + n], BS)
            dk_all[pl.ds(start, BS), :] += key_grad[n * BS : (n + 1) * BS, :]
            dv_all[pl.ds(start, BS), :] += value_grad[n * BS : (n + 1) * BS, :]

    @pl.when(step == pl.num_programs(0) - 1)
    def _():
        copies = []
        for j in (4, 5, 6, 7, 0, 1, 2, 3):
            ref = out_refs[j]
            start = pl.multiple_of((meta[1] * 4 + j) % 8 * BLOCK, BLOCK)
            for k, (total, table) in enumerate(((dk_all, key_all), (dv_all, value_all))):
                spot = pl.ds(k * BLOCK, BLOCK)
                if j < 4:
                    ref[spot, :] = total[pl.ds(start, BLOCK), :].astype(bf16)
                    continue
                slot = pl.ds((j - 4) * BLOCK, BLOCK)
                table[slot, :] = total[pl.ds(start, BLOCK), :].astype(bf16)
                copy = pltpu.make_async_copy(table.at[slot], ref.at[spot], sems.at[len(copies)])
                copy.start()
                copies.append(copy)
        for copy in copies:
            copy.wait()


def student_backward(meta, sel, queries, weights, grad_pieces, kv_blocks):
    size = BACKWARD_ROWS * BS
    return pl.pallas_call(
        student_backward_kernel,
        grid=(BLOCK // size,),
        in_specs=[
            pl.BlockSpec(memory_space=SMEM),
            pl.BlockSpec(memory_space=SMEM),
            pl.BlockSpec((size, HD), lambda i: (i, 0)),
            pl.BlockSpec((size, NSEL * BS), lambda i: (i, 0)),
            pl.BlockSpec((8, size, HD), lambda i: (0, i, 0)),
        ]
        + [ANY] * len(kv_blocks),
        out_specs=[pl.BlockSpec((size, HD), lambda i: (i, 0))] + [VMEM] * 4 + [FAR] * 4,
        out_shape=[jax.ShapeDtypeStruct((BLOCK, HD), f32)]
        + [jax.ShapeDtypeStruct((2 * BLOCK, HD), bf16)] * 4
        + [pltpu.HBM((2 * BLOCK, HD), bf16)] * 4,
        scratch_shapes=KEYS + [pltpu.SemaphoreType.DMA((16,))] + [pltpu.VMEM((8 * BLOCK, HD), f32)] * 2,
        compiler_params=pltpu.CompilerParams(vmem_limit_bytes=32 << 20),
        cost_estimate=pl.CostEstimate(
            flops=8 * BLOCK * NSEL * BS * HD, bytes_accessed=15 << 20, transcendentals=0
        ),
        name="student_backward",
    )(meta, sel, queries, far(weights), grad_pieces, *kv_blocks)


def project(where, attn, weights, width, extra=None, after=()):
    composed = len(weights) == 1

    def piece(p, at):
        return (p // 2) * 4 + at[0] * 2 + p % 2

    if composed:
        w_specs = [pl.BlockSpec((8, 1, COUNTS, 3 * HD), lambda p, c: (0, piece(p, c), 0, 0))]
    else:
        w_specs = [
            pl.BlockSpec((HD, width), lambda p, c: (0, piece(p, c))),
            pl.BlockSpec((2 * HD, width), lambda p, c: (0, piece(p, c))),
        ]
    out_spec = pl.BlockSpec((1, BLOCK, width), lambda p, c: (p, 0, 0))
    more = [] if extra is None else [extra]
    args = [far(a) for a in attn] + list(weights) + more + list(after)

    def kernel(at, s_ref, a_ref, b_ref, *refs):
        near = pl.multiple_of(at[1] * HD, HD)
        far = pl.multiple_of((1 - at[1]) * HD, HD)
        if composed:
            wide = refs[0][...].reshape(HD, 3 * HD)
            here, back = a_ref[...], b_ref[...]
            first = jnp.where(at[1] == 0, here, back)
            second = jnp.where(at[1] == 0, back, here)

            def times(value, j):
                return lax.dot_general(
                    value, wide[:, j * HD : (j + 1) * HD], ROWS_NT, preferred_element_type=f32
                )

            acc = times(s_ref[...], 0) - times(first, 1) - times(second, 2)
        else:
            acc = jnp.dot(s_ref[...], refs[0][...], preferred_element_type=f32)
            acc -= jnp.dot(a_ref[...], refs[1][pl.ds(near, HD), :], preferred_element_type=f32)
            acc -= jnp.dot(b_ref[...], refs[1][pl.ds(far, HD), :], preferred_element_type=f32)
        if extra is not None:
            acc = acc + refs[len(weights)][0].astype(f32)
        refs[-1][0] = acc.astype(bf16)

    return pl.pallas_call(
        kernel,
        grid_spec=pltpu.PrefetchScalarGridSpec(
            num_scalar_prefetch=1,
            grid=(8,),
            in_specs=[pl.BlockSpec((BLOCK, HD), lambda p, c: (0, 0))] * 3
            + w_specs
            + [out_spec] * len(more)
            + [ANY] * len(after),
            out_specs=out_spec,
        ),
        out_shape=(pltpu.HBM if more else jax.ShapeDtypeStruct)((8, BLOCK, width), bf16),
        compiler_params=pltpu.CompilerParams(vmem_limit_bytes=16 << 20),
        cost_estimate=pl.CostEstimate(
            flops=2 * 8 * BLOCK * width * 3 * HD,
            bytes_accessed=2 * 8 * BLOCK * width * (1 + len(more)) + (2 << 20),
            transcendentals=0,
        ),
        name="project_grad" if composed else "project_mismatch",
    )(where, *args)


def token(*arrays):
    total = None
    for array in arrays:
        corner = array[:COUNTS, :] if array.ndim == 2 else array[0, :COUNTS, :]
        total = corner if total is None else total + corner
    return total


def gate(values, after):
    def kernel(*refs):
        pass

    n = len(values)
    return tuple(
        pl.pallas_call(
            kernel,
            in_specs=[FAR] * n + [ANY] * len(after),
            out_specs=[FAR] * n,
            out_shape=[pltpu.HBM(v.shape, v.dtype) for v in values],
            input_output_aliases={k: k for k in range(n)},
            name="gate",
        )(*map(far, values), *after)
    )


def pack_kernel(at, seg_ref, tq_ref, tk_ref, tv_ref, sk_ref, sv_ref, so_ref, *refs):
    outs, stages, sems = refs[:6], refs[6:12], refs[12]
    s_own, t_sent, q_sent, rows, q_own, t_own = stages
    near = pl.ds(pl.multiple_of(at[0] * HD, HD), HD)
    other = pl.ds(pl.multiple_of((1 - at[0]) * HD, HD), HD)
    started = 0

    def move(source, target):
        nonlocal started
        copy = pltpu.make_async_copy(source, target, sems.at[started])
        copy.start()
        started += 1
        return copy

    keys, values, last = pl.ds(0, BLOCK), pl.ds(BLOCK, BLOCK), pl.ds(2 * BLOCK, COUNTS)
    part = pl.ds(pl.multiple_of(at[1] * COUNTS, COUNTS), COUNTS)
    coming = (
        (0, [move(sk_ref, s_own.at[keys]), move(sv_ref, s_own.at[values])]),
        (1, [move(tk_ref.at[:, other], t_sent.at[keys]), move(tv_ref.at[:, other], t_sent.at[values])]),
        (2, [move(tq_ref.at[:, other], q_sent)]),
        (3, [move(so_ref.at[part], rows)]),
        (5, [move(tk_ref.at[:, near], t_own.at[keys]), move(tv_ref.at[:, near], t_own.at[values])]),
        (4, [move(tq_ref.at[:, near], q_own)]),
    )
    found = jnp.sum((seg_ref[...] == 0).astype(f32), axis=0, keepdims=True)
    first = lax.broadcasted_iota(jnp.int32, (COUNTS, HD), 0) == 0
    counts = jnp.where(first, found, 0.0).astype(bf16)
    for stage in (s_own, t_own, t_sent):
        stage[last, :] = counts
    going = []
    for k, copies in coming:
        for copy in copies:
            copy.wait()
        going.append(move(stages[k], outs[k]))
    for copy in going:
        copy.wait()


def pack(at, seg, *arrays):
    short = (BLOCK, HD)
    shapes = [(SPAN, HD)] * 2 + [short, (COUNTS, arrays[-1].shape[1]), short, (SPAN, HD)]
    return pl.pallas_call(
        pack_kernel,
        in_specs=[pl.BlockSpec(memory_space=SMEM), VMEM] + [FAR] * 6,
        out_specs=[FAR] * 6,
        out_shape=[pltpu.HBM(shape, bf16) for shape in shapes],
        scratch_shapes=[pltpu.VMEM(shape, bf16) for shape in shapes] + [pltpu.SemaphoreType.DMA((15,))],
        compiler_params=pltpu.CompilerParams(vmem_limit_bytes=12 << 20),
        cost_estimate=pl.CostEstimate(flops=0, bytes_accessed=5 << 20, transcendentals=0),
        name="pack",
    )(at, seg, *map(far, arrays))


def repack_kernel(kept_ref, *refs):
    target, sem = refs[-3], refs[-1]
    copy = pltpu.make_async_copy(kept_ref, target.at[pl.ds(0, SPAN)], sem)
    copy.start()
    target[SPAN:, :] = refs[0][...]
    for k, ref in enumerate(refs[1:4]):
        refs[-2][k * SPAN : (k + 1) * SPAN, :] = ref[...]
    copy.wait()


def repack(kept, got, student, after):
    return pl.pallas_call(
        repack_kernel,
        in_specs=[FAR] + [VMEM] * 4 + [ANY] * len(after),
        out_specs=[VMEM] * 2,
        out_shape=[jax.ShapeDtypeStruct((k * SPAN, HD), bf16) for k in (2, 3)],
        scratch_shapes=[pltpu.SemaphoreType.DMA],
        compiler_params=pltpu.CompilerParams(vmem_limit_bytes=8 << 20),
        cost_estimate=pl.CostEstimate(flops=0, bytes_accessed=5 << 20, transcendentals=0),
        name="repack",
    )(far(kept), got, *student, *after)


def compose_kernel(rows_ref, s_ref, t_ref, *refs):
    rows = rows_ref[...]
    for ref, low, high in ((s_ref, 0, HD), (t_ref, HD, 3 * HD)):
        refs[-1][:, low:high] = lax.dot_general(
            rows, ref[...], ROWS_NT, preferred_element_type=f32
        ).astype(bf16)


def compose(rows, s_out, t_out, after):
    return pl.pallas_call(
        compose_kernel,
        in_specs=[VMEM] * 3 + [ANY] * len(after),
        out_specs=VMEM,
        out_shape=jax.ShapeDtypeStruct((rows.shape[0], 3 * HD), bf16),
        compiler_params=pltpu.CompilerParams(vmem_limit_bytes=24 << 20),
        cost_estimate=pl.CostEstimate(
            flops=2 * rows.shape[0] * 3 * HD * rows.shape[1], bytes_accessed=5 << 20, transcendentals=0
        ),
        name="compose",
    )(rows, s_out, t_out, *after)


def add_pieces_kernel(in_ref, out_ref):
    out_ref[...] = jnp.sum(in_ref[...].astype(f32), axis=0)


def add_pieces(pieces):
    count, rows, width = pieces.shape
    size = rows // 4
    return pl.pallas_call(
        add_pieces_kernel,
        grid=(4,),
        in_specs=[pl.BlockSpec((count, size, width), lambda i: (0, i, 0))],
        out_specs=pl.BlockSpec((size, width), lambda i: (i, 0)),
        out_shape=jax.ShapeDtypeStruct((rows, width), f32),
        compiler_params=pltpu.CompilerParams(vmem_limit_bytes=16 << 20),
        cost_estimate=pl.CostEstimate(flops=8 << 20, bytes_accessed=5 << 20, transcendentals=0),
        name="add_pieces",
    )(pieces)


def finish_kernel(at, *refs):
    low, across, high, (dk_ref, dv_ref) = refs[:4], refs[4], refs[5:9], refs[-2:]

    def write(parts):
        for ref, span in ((dk_ref, pl.ds(0, BLOCK)), (dv_ref, pl.ds(BLOCK, BLOCK))):
            total = parts[0][span, :].astype(f32)
            for part in parts[1:]:
                total = total + part[span, :].astype(f32)
            ref[...] = total

    @pl.when(at[0] == 0)
    def _():
        write(low + (across,))

    @pl.when(at[0] == 1)
    def _():
        write(high)


def finish(at, low, across, high, after):
    near = [pltpu.with_memory_space_constraint(part, pltpu.VMEM) for part in (*low, across, *high)]
    return pl.pallas_call(
        finish_kernel,
        in_specs=[pl.BlockSpec(memory_space=SMEM)] + [VMEM] * 9 + [ANY] * len(after),
        out_specs=[pl.BlockSpec((BLOCK, HD), lambda: (0, 0))] * 2,
        out_shape=[pltpu.HBM((BLOCK, HD), f32)] * 2,
        compiler_params=pltpu.CompilerParams(vmem_limit_bytes=16 << 20),
        cost_estimate=pl.CostEstimate(flops=4 << 20, bytes_accessed=5 << 20, transcendentals=0),
        name="finish",
    )(at, *near, *after)


def on_device(t_query, t_key, t_value, t_out, s_query, s_key, s_value, s_out, segments, selection):
    x, y, core = lax.axis_index("xlo"), lax.axis_index("y"), lax.axis_index("core")
    mine = 4 * x + y
    partner = 4 * (1 - x) + y

    def along_y(block, all_x, causal_x):
        return tuple(
            lax.ppermute(block, BLK, y_pairs(shift, all_x, causal_x)) for shift in (1, -1, 2)
        )

    to_partner = [(i, i ^ 4) for i in range(8)]
    at_x = jnp.stack([x, mine]).astype(jnp.int32)
    s_own, t_sent, q_sent, rows, q_own, t_own = pack(
        at_x, segments.reshape(8, HD), t_query, t_key, t_value, s_key, s_value, s_out
    )
    up = [(i, i + 4) for i in range(4)]
    s_near = along_y(s_own, (0,), (1,))
    t_got = lax.ppermute(t_sent, BLK, to_partner)
    s_low = lax.ppermute(s_own, BLK, up)
    t_two, s_three = repack(t_own, t_got, s_near, (token(s_low),))
    t_near = along_y(t_two, (0, 1), ())
    s_lows = lax.ppermute(s_three, BLK, up)
    q_got = lax.ppermute(q_sent, BLK, to_partner)

    rows = lax.all_gather(rows, GROUP, axis=0, tiled=True)
    through = compose(rows, s_out, t_out, (token(*t_near, s_lows, q_got),))
    through = lax.all_gather(through, BLK, axis=0, tiled=True).reshape(8, 16, HD // 8, 3 * HD)

    def place_of(block):
        step = (block + 4 - y) % 4
        return jnp.where(step == 0, 0, jnp.where(step == 3, 1, step + 1)), (block // 4 != x).astype(jnp.int32)

    spot, half = place_of(jnp.arange(8, dtype=jnp.int32))
    t_meta = jnp.concatenate([jnp.stack([mine, partner] + [0] * 6).astype(jnp.int32), 2 * spot + half])
    spot, half = place_of(selection // 16)
    sel = ((spot + 4 * half) * BLOCK + selection % 16 * BS).reshape(-1).astype(jnp.int32)
    k_pos = (selection[:, :, None] * BS + jnp.arange(BS, dtype=jnp.int32)).reshape(-1, 1, NSEL * BS)
    s_meta = jnp.stack([mine, x]).astype(jnp.int32)

    t_blocks = tuple(map(far, (t_own, t_got, *t_near)))
    away, here = teacher_attention(t_meta, q_got, q_own, t_blocks)
    back = lax.ppermute(away, BLK, to_partner)
    s_blocks = tuple(map(far, (s_own, *s_near, s_low, s_lows)))
    s_attn, weights = student_forward(s_meta, sel, s_query, k_pos, s_blocks)
    attn = (s_attn, here, back)

    this = jnp.stack([core, x]).astype(jnp.int32)
    other = jnp.stack([1 - core, x]).astype(jnp.int32)
    to_core = [(0, 1), (1, 0)]
    part = project(other, attn, (s_out, t_out), 2 * HD)
    grad = project(other, attn, (through,), HD, None, (token(part),))
    grad = lax.ppermute(grad, "core", to_core)
    grad = project(this, attn, (through,), HD, grad)
    grad = lax.all_to_all(grad, ZX, 0, 0, tiled=True)
    part = lax.ppermute(part, "core", to_core)
    part = project(this, attn, (s_out, t_out), 2 * HD, part)
    part = lax.all_to_all(part, ZX, 0, 0, tiled=True)

    out = student_backward(s_meta, sel, s_query, weights, grad, s_blocks)
    s_dq, pieces = out[0], out[1:]

    def earlier(shift, all_x, causal_x):
        pairs = []
        for i in range(2):
            for j in range(4):
                to = (j + shift) % 4
                if i in all_x or (i in causal_x and to < j):
                    pairs.append((4 * i + j, 4 * i + to))
        return pairs

    low, high = list(pieces[:4]), list(pieces[4:])
    for j, shift in ((1, -1), (2, 1), (3, 2)):
        low[j] = lax.ppermute(low[j], BLK, earlier(shift, (1,), (0,)))
    low_sum = low[0].astype(f32) + low[1].astype(f32) + low[2].astype(f32) + low[3].astype(f32)
    across = low_sum.astype(bf16)
    high = list(gate(high, (token(across),)))
    across = lax.ppermute(across, BLK, [(i + 4, i) for i in range(4)])
    for j, shift in ((1, -1), (2, 1), (3, 2)):
        high[j] = lax.ppermute(high[j], BLK, earlier(shift, (), (1,)))
    mismatch = add_pieces(part)
    s_dk, s_dv = finish(at_x, tuple(low), across, tuple(high), (token(mismatch[:, :HD]),))
    return mismatch, s_dq, s_dk, s_dv


def solution(mesh):
    fine = Mesh(mesh.devices.reshape(2, 4, 4, 2, 2), ("xlo", "y", "z", "core", "xhi"))
    data = P(BLK, GROUP)
    flat = P(GROUP, None)
    return jax.shard_map(
        on_device,
        mesh=fine,
        in_specs=(data, data, data, flat, data, data, data, flat, P(BLK), P(BLK, None)),
        out_specs=(data, data, data, data),
        check_vma=False,
    )
```

```python
import jax
import jax.numpy as jnp
from jax import lax
from jax.experimental import pallas as pl
from jax.experimental.pallas import tpu as pltpu
from jax.sharding import Mesh
from jax.sharding import PartitionSpec as P

HD = 128
BS = 64
NSEL = 16
BLOCK = 1024
COUNTS = 16
FORWARD_ROWS = 4
BACKWARD_ROWS = 4
TILE_Q = 512
TILE_K = 512
SCALE = HD ** (-0.5)
EXP_SCALE = SCALE * 1.4426950408889634
LOWEST = -1e30

BLK = ("xlo", "y")
GROUP = ("z", "core", "xhi")
ZX = ("z", "xhi")
f32 = jnp.float32
bf16 = jnp.bfloat16

SMEM = pltpu.SMEM
ANY = pl.BlockSpec(memory_space=pl.ANY)
FAR = pl.BlockSpec(memory_space=pltpu.HBM)

VMEM = pl.BlockSpec(memory_space=pltpu.VMEM)
ROWS_NT = (((1,), (1,)), ((), ()))
ROWS_TN = (((0,), (0,)), ((), ()))


def y_pairs(shift, all_x, causal_x):
    pairs = []
    for x in range(2):
        for y in range(4):
            to = (y + shift) % 4
            if x in all_x or (x in causal_x and y < to):
                pairs.append((4 * x + y, 4 * x + to))
    return pairs


def far(array):
    return pltpu.with_memory_space_constraint(array, pltpu.HBM)


SPAN = 2 * BLOCK + COUNTS


def blocks_of(refs):
    return [(ref, k * SPAN) for ref in refs for k in range(ref.shape[0] // SPAN)]


def load(blocks, key_all, value_all, counts, sems, meanwhile=None):
    copies = []

    def bring(source, target):
        copy = pltpu.make_async_copy(source, target, sems.at[len(copies)])
        copy.start()
        copies.append(copy)

    for j, (ref, at) in enumerate(blocks):
        slot = pl.ds(j * BLOCK, BLOCK)
        bring(ref.at[pl.ds(at, BLOCK)], key_all.at[slot])
        bring(ref.at[pl.ds(at + BLOCK, BLOCK)], value_all.at[slot])
        if counts is not None:
            bring(ref.at[pl.ds(at + 2 * BLOCK, COUNTS)], counts.at[pl.ds(j * COUNTS, COUNTS)])
    if meanwhile is not None:
        meanwhile()
    for copy in copies:
        copy.wait()


def border_of(counts):
    return jnp.sum(counts[...].astype(f32)).astype(jnp.int32)


KEYS = [pltpu.VMEM((8 * BLOCK, HD), bf16)] * 2
WITH_COUNTS = KEYS + [pltpu.VMEM((8 * COUNTS, HD), bf16), pltpu.SemaphoreType.DMA((24,))]


def teacher_kernel(meta, here_ref, *refs):
    blocks = blocks_of(refs[:-8])
    away_out, here_out, key_all, value_all, counts, sems, away_ref, away_sem = refs[-8:]
    away_copy = pltpu.make_async_copy(refs[1].at[pl.ds(SPAN, BLOCK)], away_ref, away_sem)
    away_copy.start()
    load(blocks, key_all, value_all, counts, sems)
    away_copy.wait()
    border = border_of(counts)
    per_block = BLOCK // TILE_K

    def one_block(q_ref, o_ref, block):
        first = block * BLOCK
        tiles = []
        for step in range(BLOCK // TILE_Q):
            q_pos = first + step * TILE_Q + lax.broadcasted_iota(jnp.int32, (TILE_Q, 1), 0)
            q_low = jnp.where(q_pos >= border, border, 0)
            tiles.append((q_ref[pl.ds(step * TILE_Q, TILE_Q), :], q_pos, q_low))

        def turn(masked, j, tile, carry):
            queries, q_pos, q_low = tile
            largest, total, acc = carry
            slot = meta[8 + j // per_block]
            start = pl.multiple_of(slot * BLOCK + (j % per_block) * TILE_K, TILE_K)
            scores = lax.dot_general(
                queries, key_all[pl.ds(start, TILE_K), :], ROWS_NT, preferred_element_type=f32
            )
            if masked:
                k_pos = j * TILE_K + lax.broadcasted_iota(jnp.int32, (1, TILE_K), 1)
                scores = jnp.where((k_pos <= q_pos) & (k_pos >= q_low), scores, LOWEST)
            new = jnp.maximum(largest, jnp.max(scores, axis=1, keepdims=True))
            factor = jnp.exp2((largest - new) * EXP_SCALE)
            weights = jnp.exp2((scores - new) * EXP_SCALE)
            total = factor * total + jnp.sum(weights, axis=1, keepdims=True)
            acc = factor * acc + jnp.dot(
                weights.astype(bf16), value_all[pl.ds(start, TILE_K), :], preferred_element_type=f32
            )
            return new, total, acc

        def turns(masked, j, carries):
            return tuple(turn(masked, j, tile, carry) for tile, carry in zip(tiles, carries))

        carries = tuple(
            (
                jnp.full((TILE_Q, 1), LOWEST, f32),
                jnp.zeros((TILE_Q, 1), f32),
                jnp.zeros((TILE_Q, HD), f32),
            )
            for _ in tiles
        )
        begin = jnp.where(first >= border, border, 0) // TILE_K
        diagonal = first // TILE_K
        low_last = jnp.where(first + BLOCK - 1 >= border, border, 0)
        clear = jnp.minimum((low_last + TILE_K - 1) // TILE_K, diagonal)
        carries = lax.fori_loop(begin, clear, lambda j, c: turns(True, j, c), carries)
        carries = lax.fori_loop(clear, diagonal, lambda j, c: turns(False, j, c), carries)
        carries = list(carries)
        for k in range(per_block):
            for n, tile in enumerate(tiles):
                if k * TILE_K < (n + 1) * TILE_Q:
                    carries[n] = turn(True, diagonal + k, tile, carries[n])
        for step, (_, total, acc) in enumerate(carries):
            o_ref[pl.ds(step * TILE_Q, TILE_Q), :] = (acc / total).astype(bf16)

    one_block(away_ref, away_out, meta[1])
    one_block(here_ref, here_out, meta[0])


def teacher_attention(meta, here, kv_blocks):
    return pl.pallas_call(
        teacher_kernel,
        in_specs=[pl.BlockSpec(memory_space=SMEM), VMEM] + [ANY] * len(kv_blocks),
        out_specs=[pl.BlockSpec((BLOCK, HD), lambda: (0, 0))] * 2,
        out_shape=[pltpu.HBM((BLOCK, HD), bf16)] * 2,
        scratch_shapes=WITH_COUNTS + [pltpu.VMEM((BLOCK, HD), bf16), pltpu.SemaphoreType.DMA],
        compiler_params=pltpu.CompilerParams(vmem_limit_bytes=24 << 20),
        cost_estimate=pl.CostEstimate(
            flops=8 * 4 * BLOCK * BLOCK * HD, bytes_accessed=5 << 20, transcendentals=8 * BLOCK * BLOCK
        ),
        name="teacher_attention",
    )(meta, here, *kv_blocks)


def chosen_rows(sel, row, table):
    pieces = []
    for n in range(NSEL):
        start = pl.multiple_of(sel[row * NSEL + n], BS)
        pieces.append(table[pl.ds(start, BS), :])
    return jnp.concatenate(pieces, axis=0)


def student_forward_kernel(meta, sel, q_ref, kpos_ref, *refs):
    blocks = blocks_of(refs[:-6])
    o_ref, p_ref, key_all, value_all, counts, sems = refs[-6:]
    step = pl.program_id(0)

    @pl.when(step == 0)
    def _():
        load(blocks, key_all, value_all, counts, sems)

    border = border_of(counts)
    for u in range(FORWARD_ROWS):
        row = step * FORWARD_ROWS + u
        span = pl.ds(u * BS, BS)
        q_pos = meta[0] * BLOCK + row * BS + lax.broadcasted_iota(jnp.int32, (BS, 1), 0)
        q_low = jnp.where(q_pos >= border, border, 0)
        k_pos = kpos_ref[u]
        scores = lax.dot_general(
            q_ref[span, :], chosen_rows(sel, row, key_all), ROWS_NT, preferred_element_type=f32
        )
        scores = jnp.where((k_pos <= q_pos) & (k_pos >= q_low), scores, LOWEST)
        weights = jnp.exp2((scores - jnp.max(scores, axis=1, keepdims=True)) * EXP_SCALE)
        inverse = 1.0 / jnp.sum(weights, axis=1, keepdims=True)
        p_ref[span, :] = weights * inverse
        blended = jnp.dot(
            weights.astype(bf16), chosen_rows(sel, row, value_all), preferred_element_type=f32
        )
        o_ref[span, :] = (blended * inverse).astype(bf16)


def student_forward(meta, sel, queries, k_pos, kv_blocks):
    size = FORWARD_ROWS * BS
    return pl.pallas_call(
        student_forward_kernel,
        grid=(BLOCK // size,),
        in_specs=[
            pl.BlockSpec(memory_space=SMEM),
            pl.BlockSpec(memory_space=SMEM),
            pl.BlockSpec((size, HD), lambda i: (i, 0)),
            pl.BlockSpec((FORWARD_ROWS, 1, NSEL * BS), lambda i: (i, 0, 0)),
        ]
        + [ANY] * len(kv_blocks),
        out_specs=[
            pl.BlockSpec((size, HD), lambda i: (i, 0)),
            pl.BlockSpec((size, NSEL * BS), lambda i: (i, 0)),
        ],
        out_shape=[
            pltpu.HBM((BLOCK, HD), bf16),
            pltpu.HBM((BLOCK, NSEL * BS), f32),
        ],
        scratch_shapes=WITH_COUNTS,
        compiler_params=pltpu.CompilerParams(vmem_limit_bytes=24 << 20),
        cost_estimate=pl.CostEstimate(
            flops=4 * BLOCK * NSEL * BS * HD, bytes_accessed=9 << 20, transcendentals=BLOCK * NSEL * BS
        ),
        name="student_forward",
    )(meta, sel, queries, k_pos, *kv_blocks)


def student_backward_kernel(meta, sel, q_ref, p_ref, g_ref, *refs):
    blocks = blocks_of(refs[:-14])
    dq_ref, out_refs = refs[-14], refs[-13:-5]
    key_all, value_all, sems, dk_all, dv_all = refs[-5:]
    step = pl.program_id(0)

    @pl.when(step == 0)
    def _():
        def clear():
            dk_all[...] = jnp.zeros_like(dk_all)
            dv_all[...] = jnp.zeros_like(dv_all)

        load(blocks, key_all, value_all, None, sems, clear)

    for u in range(BACKWARD_ROWS):
        row = step * BACKWARD_ROWS + u
        span = pl.ds(u * BS, BS)
        grad = jnp.sum(g_ref[:, span, :].astype(f32), axis=0).astype(bf16)
        weights = p_ref[span, :]
        weight_grad = lax.dot_general(
            grad, chosen_rows(sel, row, value_all), ROWS_NT, preferred_element_type=f32
        )
        row_dots = jnp.sum(weights * weight_grad, axis=1, keepdims=True)
        score_grad = (weights * (weight_grad - row_dots) * SCALE).astype(bf16)
        dq_ref[span, :] = jnp.dot(
            score_grad, chosen_rows(sel, row, key_all), preferred_element_type=f32
        )
        key_grad = lax.dot_general(score_grad, q_ref[span, :], ROWS_TN, preferred_element_type=f32)
        value_grad = lax.dot_general(
            weights.astype(bf16), grad, ROWS_TN, preferred_element_type=f32
        )
        for n in range(NSEL):
            start = pl.multiple_of(sel[row * NSEL + n], BS)
            dk_all[pl.ds(start, BS), :] += key_grad[n * BS : (n + 1) * BS, :]
            dv_all[pl.ds(start, BS), :] += value_grad[n * BS : (n + 1) * BS, :]

    @pl.when(step == pl.num_programs(0) - 1)
    def _():
        copies = []
        for j in (4, 5, 6, 7, 0, 1, 2, 3):
            ref = out_refs[j]
            start = pl.multiple_of((meta[1] * 4 + j) % 8 * BLOCK, BLOCK)
            for k, (total, table) in enumerate(((dk_all, key_all), (dv_all, value_all))):
                spot = pl.ds(k * BLOCK, BLOCK)
                if j < 4:
                    ref[spot, :] = total[pl.ds(start, BLOCK), :].astype(bf16)
                    continue
                slot = pl.ds((j - 4) * BLOCK, BLOCK)
                table[slot, :] = total[pl.ds(start, BLOCK), :].astype(bf16)
                copy = pltpu.make_async_copy(table.at[slot], ref.at[spot], sems.at[len(copies)])
                copy.start()
                copies.append(copy)
        for copy in copies:
            copy.wait()


def student_backward(meta, sel, queries, weights, grad_pieces, kv_blocks):
    size = BACKWARD_ROWS * BS
    return pl.pallas_call(
        student_backward_kernel,
        grid=(BLOCK // size,),
        in_specs=[
            pl.BlockSpec(memory_space=SMEM),
            pl.BlockSpec(memory_space=SMEM),
            pl.BlockSpec((size, HD), lambda i: (i, 0)),
            pl.BlockSpec((size, NSEL * BS), lambda i: (i, 0)),
            pl.BlockSpec((8, size, HD), lambda i: (0, i, 0)),
        ]
        + [ANY] * len(kv_blocks),
        out_specs=[pl.BlockSpec((size, HD), lambda i: (i, 0))] + [VMEM] * 4 + [FAR] * 4,
        out_shape=[jax.ShapeDtypeStruct((BLOCK, HD), f32)]
        + [jax.ShapeDtypeStruct((2 * BLOCK, HD), bf16)] * 4
        + [pltpu.HBM((2 * BLOCK, HD), bf16)] * 4,
        scratch_shapes=KEYS + [pltpu.SemaphoreType.DMA((16,))] + [pltpu.VMEM((8 * BLOCK, HD), f32)] * 2,
        compiler_params=pltpu.CompilerParams(vmem_limit_bytes=32 << 20),
        cost_estimate=pl.CostEstimate(
            flops=8 * BLOCK * NSEL * BS * HD, bytes_accessed=15 << 20, transcendentals=0
        ),
        name="student_backward",
    )(meta, sel, queries, far(weights), grad_pieces, *kv_blocks)


def project(where, attn, weights, width, extra=None, after=()):
    composed = len(weights) == 1

    def piece(p, at):
        return (p // 2) * 4 + at[0] * 2 + p % 2

    if composed:
        w_specs = [pl.BlockSpec((8, 1, COUNTS, 3 * HD), lambda p, c: (0, piece(p, c), 0, 0))]
    else:
        w_specs = [
            pl.BlockSpec((HD, width), lambda p, c: (0, piece(p, c))),
            pl.BlockSpec((2 * HD, width), lambda p, c: (0, piece(p, c))),
        ]
    out_spec = pl.BlockSpec((1, BLOCK, width), lambda p, c: (p, 0, 0))
    more = [] if extra is None else [extra]
    args = [far(a) for a in attn] + list(weights) + more + list(after)

    def kernel(at, s_ref, a_ref, b_ref, *refs):
        near = pl.multiple_of(at[1] * HD, HD)
        far = pl.multiple_of((1 - at[1]) * HD, HD)
        if composed:
            wide = refs[0][...].reshape(HD, 3 * HD)
            here, back = a_ref[...], b_ref[...]
            first = jnp.where(at[1] == 0, here, back)
            second = jnp.where(at[1] == 0, back, here)

            def times(value, j):
                return lax.dot_general(
                    value, wide[:, j * HD : (j + 1) * HD], ROWS_NT, preferred_element_type=f32
                )

            acc = times(s_ref[...], 0) - times(first, 1) - times(second, 2)
        else:
            acc = jnp.dot(s_ref[...], refs[0][...], preferred_element_type=f32)
            acc -= jnp.dot(a_ref[...], refs[1][pl.ds(near, HD), :], preferred_element_type=f32)
            acc -= jnp.dot(b_ref[...], refs[1][pl.ds(far, HD), :], preferred_element_type=f32)
        if extra is not None:
            acc = acc + refs[len(weights)][0].astype(f32)
        refs[-1][0] = acc.astype(bf16)

    return pl.pallas_call(
        kernel,
        grid_spec=pltpu.PrefetchScalarGridSpec(
            num_scalar_prefetch=1,
            grid=(8,),
            in_specs=[pl.BlockSpec((BLOCK, HD), lambda p, c: (0, 0))] * 3
            + w_specs
            + [out_spec] * len(more)
            + [ANY] * len(after),
            out_specs=out_spec,
        ),
        out_shape=(pltpu.HBM if more else jax.ShapeDtypeStruct)((8, BLOCK, width), bf16),
        compiler_params=pltpu.CompilerParams(vmem_limit_bytes=16 << 20),
        cost_estimate=pl.CostEstimate(
            flops=2 * 8 * BLOCK * width * 3 * HD,
            bytes_accessed=2 * 8 * BLOCK * width * (1 + len(more)) + (2 << 20),
            transcendentals=0,
        ),
        name="project_grad" if composed else "project_mismatch",
    )(where, *args)


def token(*arrays):
    total = None
    for array in arrays:
        corner = array[:COUNTS, :] if array.ndim == 2 else array[0, :COUNTS, :]
        total = corner if total is None else total + corner
    return total


def gate(values, after):
    def kernel(*refs):
        pass

    n = len(values)
    return tuple(
        pl.pallas_call(
            kernel,
            in_specs=[FAR] * n + [ANY] * len(after),
            out_specs=[FAR] * n,
            out_shape=[pltpu.HBM(v.shape, v.dtype) for v in values],
            input_output_aliases={k: k for k in range(n)},
            name="gate",
        )(*map(far, values), *after)
    )


def pack_kernel(at, seg_ref, tq_ref, tk_ref, tv_ref, sk_ref, sv_ref, so_ref, *refs):
    outs, stages, sems = refs[:5], refs[5:10], refs[10]
    s_own, t_sent, rows, q_own, t_own = stages
    near = pl.ds(pl.multiple_of(at[0] * HD, HD), HD)
    other = pl.ds(pl.multiple_of((1 - at[0]) * HD, HD), HD)
    started = 0

    def move(source, target):
        nonlocal started
        copy = pltpu.make_async_copy(source, target, sems.at[started])
        copy.start()
        started += 1
        return copy

    keys, values, last = pl.ds(0, BLOCK), pl.ds(BLOCK, BLOCK), pl.ds(2 * BLOCK, COUNTS)
    part = pl.ds(pl.multiple_of(at[1] * COUNTS, COUNTS), COUNTS)
    more = pl.ds(SPAN, BLOCK)
    coming = (
        (0, [move(sk_ref, s_own.at[keys]), move(sv_ref, s_own.at[values])]),
        (
            1,
            [
                move(tk_ref.at[:, other], t_sent.at[keys]),
                move(tv_ref.at[:, other], t_sent.at[values]),
                move(tq_ref.at[:, other], t_sent.at[more]),
            ],
        ),
        (2, [move(so_ref.at[part], rows)]),
        (4, [move(tk_ref.at[:, near], t_own.at[keys]), move(tv_ref.at[:, near], t_own.at[values])]),
        (3, [move(tq_ref.at[:, near], q_own)]),
    )
    found = jnp.sum((seg_ref[...] == 0).astype(f32), axis=0, keepdims=True)
    first = lax.broadcasted_iota(jnp.int32, (COUNTS, HD), 0) == 0
    counts = jnp.where(first, found, 0.0).astype(bf16)
    for stage in (s_own, t_own, t_sent):
        stage[last, :] = counts
    going = []
    for k, copies in coming:
        for copy in copies:
            copy.wait()
        going.append(move(stages[k], outs[k]))
    for copy in going:
        copy.wait()


def pack(at, seg, *arrays):
    short = (BLOCK, HD)
    span = (SPAN, HD)
    shapes = [span, (SPAN + BLOCK, HD), (COUNTS, arrays[-1].shape[1]), short, span]
    return pl.pallas_call(
        pack_kernel,
        in_specs=[pl.BlockSpec(memory_space=SMEM), VMEM] + [FAR] * 6,
        out_specs=[FAR] * 5,
        out_shape=[pltpu.HBM(shape, bf16) for shape in shapes],
        scratch_shapes=[pltpu.VMEM(shape, bf16) for shape in shapes] + [pltpu.SemaphoreType.DMA((14,))],
        compiler_params=pltpu.CompilerParams(vmem_limit_bytes=12 << 20),
        cost_estimate=pl.CostEstimate(flops=0, bytes_accessed=5 << 20, transcendentals=0),
        name="pack",
    )(at, seg, *map(far, arrays))


def repack_kernel(kept_ref, *refs):
    target, sem = refs[-3], refs[-1]
    copy = pltpu.make_async_copy(kept_ref, target.at[pl.ds(0, SPAN)], sem)
    copy.start()
    target[SPAN:, :] = refs[0][:SPAN, :]
    for k, ref in enumerate(refs[1:4]):
        refs[-2][k * SPAN : (k + 1) * SPAN, :] = ref[...]
    copy.wait()


def repack(kept, got, student, after):
    return pl.pallas_call(
        repack_kernel,
        in_specs=[FAR] + [VMEM] * 4 + [ANY] * len(after),
        out_specs=[VMEM] * 2,
        out_shape=[jax.ShapeDtypeStruct((k * SPAN, HD), bf16) for k in (2, 3)],
        scratch_shapes=[pltpu.SemaphoreType.DMA],
        compiler_params=pltpu.CompilerParams(vmem_limit_bytes=8 << 20),
        cost_estimate=pl.CostEstimate(flops=0, bytes_accessed=5 << 20, transcendentals=0),
        name="repack",
    )(far(kept), got, *student, *after)


def compose_kernel(rows_ref, s_ref, t_ref, *refs):
    rows = rows_ref[...]
    for ref, low, high in ((s_ref, 0, HD), (t_ref, HD, 3 * HD)):
        refs[-1][:, low:high] = lax.dot_general(
            rows, ref[...], ROWS_NT, preferred_element_type=f32
        ).astype(bf16)


def compose(rows, s_out, t_out, after):
    return pl.pallas_call(
        compose_kernel,
        in_specs=[VMEM] * 3 + [ANY] * len(after),
        out_specs=VMEM,
        out_shape=jax.ShapeDtypeStruct((rows.shape[0], 3 * HD), bf16),
        compiler_params=pltpu.CompilerParams(vmem_limit_bytes=24 << 20),
        cost_estimate=pl.CostEstimate(
            flops=2 * rows.shape[0] * 3 * HD * rows.shape[1], bytes_accessed=5 << 20, transcendentals=0
        ),
        name="compose",
    )(rows, s_out, t_out, *after)


def add_pieces_kernel(in_ref, out_ref):
    out_ref[...] = jnp.sum(in_ref[...].astype(f32), axis=0)


def add_pieces(pieces):
    count, rows, width = pieces.shape
    size = rows // 4
    return pl.pallas_call(
        add_pieces_kernel,
        grid=(4,),
        in_specs=[pl.BlockSpec((count, size, width), lambda i: (0, i, 0))],
        out_specs=pl.BlockSpec((size, width), lambda i: (i, 0)),
        out_shape=jax.ShapeDtypeStruct((rows, width), f32),
        compiler_params=pltpu.CompilerParams(vmem_limit_bytes=16 << 20),
        cost_estimate=pl.CostEstimate(flops=8 << 20, bytes_accessed=5 << 20, transcendentals=0),
        name="add_pieces",
    )(pieces)


def finish_kernel(at, *refs):
    low, across, high, (dk_ref, dv_ref) = refs[:4], refs[4], refs[5:9], refs[-2:]

    def write(parts):
        for ref, span in ((dk_ref, pl.ds(0, BLOCK)), (dv_ref, pl.ds(BLOCK, BLOCK))):
            total = parts[0][span, :].astype(f32)
            for part in parts[1:]:
                total = total + part[span, :].astype(f32)
            ref[...] = total

    @pl.when(at[0] == 0)
    def _():
        write(low + (across,))

    @pl.when(at[0] == 1)
    def _():
        write(high)


def finish(at, low, across, high, after):
    near = [pltpu.with_memory_space_constraint(part, pltpu.VMEM) for part in (*low, across, *high)]
    return pl.pallas_call(
        finish_kernel,
        in_specs=[pl.BlockSpec(memory_space=SMEM)] + [VMEM] * 9 + [ANY] * len(after),
        out_specs=[pl.BlockSpec((BLOCK, HD), lambda: (0, 0))] * 2,
        out_shape=[pltpu.HBM((BLOCK, HD), f32)] * 2,
        compiler_params=pltpu.CompilerParams(vmem_limit_bytes=16 << 20),
        cost_estimate=pl.CostEstimate(flops=4 << 20, bytes_accessed=5 << 20, transcendentals=0),
        name="finish",
    )(at, *near, *after)


def on_device(t_query, t_key, t_value, t_out, s_query, s_key, s_value, s_out, segments, selection):
    x, y, core = lax.axis_index("xlo"), lax.axis_index("y"), lax.axis_index("core")
    mine = 4 * x + y
    partner = 4 * (1 - x) + y

    def along_y(block, all_x, causal_x):
        return tuple(
            lax.ppermute(block, BLK, y_pairs(shift, all_x, causal_x)) for shift in (1, -1, 2)
        )

    to_partner = [(i, i ^ 4) for i in range(8)]
    at_x = jnp.stack([x, mine]).astype(jnp.int32)
    s_own, t_sent, rows, q_own, t_own = pack(
        at_x, segments.reshape(8, HD), t_query, t_key, t_value, s_key, s_value, s_out
    )
    up = [(i, i + 4) for i in range(4)]
    s_near = along_y(s_own, (0,), (1,))
    t_got = lax.ppermute(t_sent, BLK, to_partner)
    s_low = lax.ppermute(s_own, BLK, up)
    t_two, s_three = repack(t_own, t_got, s_near, (token(s_low),))
    t_near = along_y(t_two, (0, 1), ())
    s_lows = lax.ppermute(s_three, BLK, up)

    def place_of(block):
        step = (block + 4 - y) % 4
        return jnp.where(step == 0, 0, jnp.where(step == 3, 1, step + 1)), (block // 4 != x).astype(jnp.int32)

    spot, half = place_of(jnp.arange(8, dtype=jnp.int32))
    t_meta = jnp.concatenate([jnp.stack([mine, partner] + [0] * 6).astype(jnp.int32), 2 * spot + half])
    spot, half = place_of(selection // 16)
    sel = ((spot + 4 * half) * BLOCK + selection % 16 * BS).reshape(-1).astype(jnp.int32)
    k_pos = (selection[:, :, None] * BS + jnp.arange(BS, dtype=jnp.int32)).reshape(-1, 1, NSEL * BS)
    s_meta = jnp.stack([mine, x]).astype(jnp.int32)

    s_blocks = tuple(map(far, (s_own, *s_near, s_low, s_lows)))
    s_attn, weights = student_forward(s_meta, sel, s_query, k_pos, s_blocks)

    rows = lax.all_gather(rows, GROUP, axis=0, tiled=True)
    through = compose(rows, s_out, t_out, (token(*t_near, s_attn),))
    through = lax.all_gather(through, BLK, axis=0, tiled=True).reshape(8, 16, HD // 8, 3 * HD)

    t_blocks = tuple(map(far, (t_own, t_got, *t_near)))
    away, here = teacher_attention(t_meta, q_own, t_blocks)
    back = lax.ppermute(away, BLK, to_partner)
    attn = (s_attn, here, back)

    this = jnp.stack([core, x]).astype(jnp.int32)
    other = jnp.stack([1 - core, x]).astype(jnp.int32)
    to_core = [(0, 1), (1, 0)]
    part = project(other, attn, (s_out, t_out), 2 * HD)
    grad = project(other, attn, (through,), HD, None, (token(part),))
    grad = lax.ppermute(grad, "core", to_core)
    grad = project(this, attn, (through,), HD, grad)
    grad = lax.all_to_all(grad, ZX, 0, 0, tiled=True)
    part = lax.ppermute(part, "core", to_core)
    part = project(this, attn, (s_out, t_out), 2 * HD, part)
    part = lax.all_to_all(part, ZX, 0, 0, tiled=True)

    out = student_backward(s_meta, sel, s_query, weights, grad, s_blocks)
    s_dq, pieces = out[0], out[1:]

    def earlier(shift, all_x, causal_x):
        pairs = []
        for i in range(2):
            for j in range(4):
                to = (j + shift) % 4
                if i in all_x or (i in causal_x and to < j):
                    pairs.append((4 * i + j, 4 * i + to))
        return pairs

    low, high = list(pieces[:4]), list(pieces[4:])
    for j, shift in ((1, -1), (2, 1), (3, 2)):
        low[j] = lax.ppermute(low[j], BLK, earlier(shift, (1,), (0,)))
    low_sum = low[0].astype(f32) + low[1].astype(f32) + low[2].astype(f32) + low[3].astype(f32)
    across = low_sum.astype(bf16)
    high = list(gate(high, (token(across),)))
    across = lax.ppermute(across, BLK, [(i + 4, i) for i in range(4)])
    for j, shift in ((1, -1), (2, 1), (3, 2)):
        high[j] = lax.ppermute(high[j], BLK, earlier(shift, (), (1,)))
    mismatch = add_pieces(part)
    s_dk, s_dv = finish(at_x, tuple(low), across, tuple(high), (token(mismatch[:, :HD]),))
    return mismatch, s_dq, s_dk, s_dv


def solution(mesh):
    fine = Mesh(mesh.devices.reshape(2, 4, 4, 2, 2), ("xlo", "y", "z", "core", "xhi"))
    data = P(BLK, GROUP)
    flat = P(GROUP, None)
    return jax.shard_map(
        on_device,
        mesh=fine,
        in_specs=(data, data, data, flat, data, data, data, flat, P(BLK), P(BLK, None)),
        out_specs=(data, data, data, data),
        check_vma=False,
    )
```

```python
import jax
import jax.numpy as jnp
from jax import lax
from jax.experimental import pallas as pl
from jax.experimental.pallas import tpu as pltpu
from jax.sharding import Mesh
from jax.sharding import PartitionSpec as P

HD = 128
BS = 64
NSEL = 16
BLOCK = 1024
COUNTS = 16
FORWARD_ROWS = 4
BACKWARD_ROWS = 4
TILE_Q = 512
TILE_K = 512
SCALE = HD ** (-0.5)
EXP_SCALE = SCALE * 1.4426950408889634
LOWEST = -1e30

BLK = ("xlo", "y")
GROUP = ("z", "core", "xhi")
ZX = ("z", "xhi")
f32 = jnp.float32
bf16 = jnp.bfloat16

SMEM = pltpu.SMEM
ANY = pl.BlockSpec(memory_space=pl.ANY)
FAR = pl.BlockSpec(memory_space=pltpu.HBM)

VMEM = pl.BlockSpec(memory_space=pltpu.VMEM)
ROWS_NT = (((1,), (1,)), ((), ()))
ROWS_TN = (((0,), (0,)), ((), ()))


def y_pairs(shift, all_x, causal_x):
    pairs = []
    for x in range(2):
        for y in range(4):
            to = (y + shift) % 4
            if x in all_x or (x in causal_x and y < to):
                pairs.append((4 * x + y, 4 * x + to))
    return pairs


def far(array):
    return pltpu.with_memory_space_constraint(array, pltpu.HBM)


SPAN = 2 * BLOCK + COUNTS


def blocks_of(refs):
    return [(ref, k * SPAN) for ref in refs for k in range(ref.shape[0] // SPAN)]


def load(blocks, key_all, value_all, counts, sems, meanwhile=None):
    copies = []

    def bring(source, target):
        copy = pltpu.make_async_copy(source, target, sems.at[len(copies)])
        copy.start()
        copies.append(copy)

    for j, (ref, at) in enumerate(blocks):
        slot = pl.ds(j * BLOCK, BLOCK)
        bring(ref.at[pl.ds(at, BLOCK)], key_all.at[slot])
        bring(ref.at[pl.ds(at + BLOCK, BLOCK)], value_all.at[slot])
        if counts is not None:
            bring(ref.at[pl.ds(at + 2 * BLOCK, COUNTS)], counts.at[pl.ds(j * COUNTS, COUNTS)])
    if meanwhile is not None:
        meanwhile()
    for copy in copies:
        copy.wait()


def border_of(counts):
    return jnp.sum(counts[...].astype(f32)).astype(jnp.int32)


KEYS = [pltpu.VMEM((8 * BLOCK, HD), bf16)] * 2
WITH_COUNTS = KEYS + [pltpu.VMEM((8 * COUNTS, HD), bf16), pltpu.SemaphoreType.DMA((24,))]


def teacher_kernel(meta, here_ref, *refs):
    blocks = blocks_of(refs[:-8])
    away_out, here_out, key_all, value_all, counts, sems, away_ref, away_sem = refs[-8:]
    away_copy = pltpu.make_async_copy(refs[1].at[pl.ds(SPAN, BLOCK)], away_ref, away_sem)
    away_copy.start()
    load(blocks, key_all, value_all, counts, sems)
    away_copy.wait()
    border = border_of(counts)
    per_block = BLOCK // TILE_K

    def one_block(q_ref, o_ref, block):
        first = block * BLOCK
        tiles = []
        for step in range(BLOCK // TILE_Q):
            q_pos = first + step * TILE_Q + lax.broadcasted_iota(jnp.int32, (TILE_Q, 1), 0)
            q_low = jnp.where(q_pos >= border, border, 0)
            tiles.append((q_ref[pl.ds(step * TILE_Q, TILE_Q), :], q_pos, q_low))

        def turn(masked, j, tile, carry):
            queries, q_pos, q_low = tile
            largest, total, acc = carry
            slot = meta[8 + j // per_block]
            start = pl.multiple_of(slot * BLOCK + (j % per_block) * TILE_K, TILE_K)
            scores = lax.dot_general(
                queries, key_all[pl.ds(start, TILE_K), :], ROWS_NT, preferred_element_type=f32
            )
            if masked:
                k_pos = j * TILE_K + lax.broadcasted_iota(jnp.int32, (1, TILE_K), 1)
                scores = jnp.where((k_pos <= q_pos) & (k_pos >= q_low), scores, LOWEST)
            new = jnp.maximum(largest, jnp.max(scores, axis=1, keepdims=True))
            factor = jnp.exp2((largest - new) * EXP_SCALE)
            weights = jnp.exp2((scores - new) * EXP_SCALE)
            total = factor * total + jnp.sum(weights, axis=1, keepdims=True)
            acc = factor * acc + jnp.dot(
                weights.astype(bf16), value_all[pl.ds(start, TILE_K), :], preferred_element_type=f32
            )
            return new, total, acc

        def turns(masked, j, carries):
            return tuple(turn(masked, j, tile, carry) for tile, carry in zip(tiles, carries))

        carries = tuple(
            (
                jnp.full((TILE_Q, 1), LOWEST, f32),
                jnp.zeros((TILE_Q, 1), f32),
                jnp.zeros((TILE_Q, HD), f32),
            )
            for _ in tiles
        )
        begin = jnp.where(first >= border, border, 0) // TILE_K
        diagonal = first // TILE_K
        low_last = jnp.where(first + BLOCK - 1 >= border, border, 0)
        clear = jnp.minimum((low_last + TILE_K - 1) // TILE_K, diagonal)
        carries = lax.fori_loop(begin, clear, lambda j, c: turns(True, j, c), carries)
        carries = lax.fori_loop(clear, diagonal, lambda j, c: turns(False, j, c), carries)
        carries = list(carries)
        for k in range(per_block):
            for n, tile in enumerate(tiles):
                if k * TILE_K < (n + 1) * TILE_Q:
                    carries[n] = turn(True, diagonal + k, tile, carries[n])
        for step, (_, total, acc) in enumerate(carries):
            o_ref[pl.ds(step * TILE_Q, TILE_Q), :] = (acc / total).astype(bf16)

    one_block(away_ref, away_out, meta[1])
    one_block(here_ref, here_out, meta[0])


def teacher_attention(meta, here, kv_blocks):
    return pl.pallas_call(
        teacher_kernel,
        in_specs=[pl.BlockSpec(memory_space=SMEM), pl.BlockSpec((BLOCK, HD), lambda: (0, 0))]
        + [ANY] * len(kv_blocks),
        out_specs=[pl.BlockSpec((BLOCK, HD), lambda: (0, 0))] * 2,
        out_shape=[pltpu.HBM((BLOCK, HD), bf16)] * 2,
        scratch_shapes=WITH_COUNTS + [pltpu.VMEM((BLOCK, HD), bf16), pltpu.SemaphoreType.DMA],
        compiler_params=pltpu.CompilerParams(vmem_limit_bytes=24 << 20),
        cost_estimate=pl.CostEstimate(
            flops=8 * 4 * BLOCK * BLOCK * HD, bytes_accessed=5 << 20, transcendentals=8 * BLOCK * BLOCK
        ),
        name="teacher_attention",
    )(meta, far(here), *kv_blocks)


def chosen_rows(sel, row, table):
    pieces = []
    for n in range(NSEL):
        start = pl.multiple_of(sel[row * NSEL + n], BS)
        pieces.append(table[pl.ds(start, BS), :])
    return jnp.concatenate(pieces, axis=0)


def student_forward_kernel(meta, sel, q_ref, kpos_ref, *refs):
    blocks = blocks_of(refs[:-6])
    o_ref, p_ref, key_all, value_all, counts, sems = refs[-6:]
    step = pl.program_id(0)

    @pl.when(step == 0)
    def _():
        load(blocks, key_all, value_all, counts, sems)

    border = border_of(counts)
    for u in range(FORWARD_ROWS):
        row = step * FORWARD_ROWS + u
        span = pl.ds(u * BS, BS)
        q_pos = meta[0] * BLOCK + row * BS + lax.broadcasted_iota(jnp.int32, (BS, 1), 0)
        q_low = jnp.where(q_pos >= border, border, 0)
        k_pos = kpos_ref[u]
        scores = lax.dot_general(
            q_ref[span, :], chosen_rows(sel, row, key_all), ROWS_NT, preferred_element_type=f32
        )
        scores = jnp.where((k_pos <= q_pos) & (k_pos >= q_low), scores, LOWEST)
        weights = jnp.exp2((scores - jnp.max(scores, axis=1, keepdims=True)) * EXP_SCALE)
        inverse = 1.0 / jnp.sum(weights, axis=1, keepdims=True)
        p_ref[span, :] = weights * inverse
        blended = jnp.dot(
            weights.astype(bf16), chosen_rows(sel, row, value_all), preferred_element_type=f32
        )
        o_ref[span, :] = (blended * inverse).astype(bf16)


def student_forward(meta, sel, queries, k_pos, kv_blocks):
    size = FORWARD_ROWS * BS
    return pl.pallas_call(
        student_forward_kernel,
        grid=(BLOCK // size,),
        in_specs=[
            pl.BlockSpec(memory_space=SMEM),
            pl.BlockSpec(memory_space=SMEM),
            pl.BlockSpec((size, HD), lambda i: (i, 0)),
            pl.BlockSpec((FORWARD_ROWS, 1, NSEL * BS), lambda i: (i, 0, 0)),
        ]
        + [ANY] * len(kv_blocks),
        out_specs=[
            pl.BlockSpec((size, HD), lambda i: (i, 0)),
            pl.BlockSpec((size, NSEL * BS), lambda i: (i, 0)),
        ],
        out_shape=[
            pltpu.HBM((BLOCK, HD), bf16),
            pltpu.HBM((BLOCK, NSEL * BS), f32),
        ],
        scratch_shapes=WITH_COUNTS,
        compiler_params=pltpu.CompilerParams(vmem_limit_bytes=24 << 20),
        cost_estimate=pl.CostEstimate(
            flops=4 * BLOCK * NSEL * BS * HD, bytes_accessed=9 << 20, transcendentals=BLOCK * NSEL * BS
        ),
        name="student_forward",
    )(meta, sel, queries, k_pos, *kv_blocks)


def student_backward_kernel(meta, sel, q_ref, p_ref, g_ref, *refs):
    blocks = blocks_of(refs[:-14])
    dq_ref, out_refs = refs[-14], refs[-13:-5]
    key_all, value_all, sems, dk_all, dv_all = refs[-5:]
    step = pl.program_id(0)

    @pl.when(step == 0)
    def _():
        def clear():
            dk_all[...] = jnp.zeros_like(dk_all)
            dv_all[...] = jnp.zeros_like(dv_all)

        load(blocks, key_all, value_all, None, sems, clear)

    for u in range(BACKWARD_ROWS):
        row = step * BACKWARD_ROWS + u
        span = pl.ds(u * BS, BS)
        grad = jnp.sum(g_ref[:, span, :].astype(f32), axis=0).astype(bf16)
        weights = p_ref[span, :]
        weight_grad = lax.dot_general(
            grad, chosen_rows(sel, row, value_all), ROWS_NT, preferred_element_type=f32
        )
        row_dots = jnp.sum(weights * weight_grad, axis=1, keepdims=True)
        score_grad = (weights * (weight_grad - row_dots) * SCALE).astype(bf16)
        dq_ref[span, :] = jnp.dot(
            score_grad, chosen_rows(sel, row, key_all), preferred_element_type=f32
        )
        key_grad = lax.dot_general(score_grad, q_ref[span, :], ROWS_TN, preferred_element_type=f32)
        value_grad = lax.dot_general(
            weights.astype(bf16), grad, ROWS_TN, preferred_element_type=f32
        )
        for n in range(NSEL):
            start = pl.multiple_of(sel[row * NSEL + n], BS)
            dk_all[pl.ds(start, BS), :] += key_grad[n * BS : (n + 1) * BS, :]
            dv_all[pl.ds(start, BS), :] += value_grad[n * BS : (n + 1) * BS, :]

    @pl.when(step == pl.num_programs(0) - 1)
    def _():
        copies = []
        for j in (4, 5, 6, 7, 0, 1, 2, 3):
            ref = out_refs[j]
            start = pl.multiple_of((meta[1] * 4 + j) % 8 * BLOCK, BLOCK)
            for k, (total, table) in enumerate(((dk_all, key_all), (dv_all, value_all))):
                spot = pl.ds(k * BLOCK, BLOCK)
                if j < 4:
                    ref[spot, :] = total[pl.ds(start, BLOCK), :].astype(bf16)
                    continue
                slot = pl.ds((j - 4) * BLOCK, BLOCK)
                table[slot, :] = total[pl.ds(start, BLOCK), :].astype(bf16)
                copy = pltpu.make_async_copy(table.at[slot], ref.at[spot], sems.at[len(copies)])
                copy.start()
                copies.append(copy)
        for copy in copies:
            copy.wait()


def student_backward(meta, sel, queries, weights, grad_pieces, kv_blocks):
    size = BACKWARD_ROWS * BS
    return pl.pallas_call(
        student_backward_kernel,
        grid=(BLOCK // size,),
        in_specs=[
            pl.BlockSpec(memory_space=SMEM),
            pl.BlockSpec(memory_space=SMEM),
            pl.BlockSpec((size, HD), lambda i: (i, 0)),
            pl.BlockSpec((size, NSEL * BS), lambda i: (i, 0)),
            pl.BlockSpec((8, size, HD), lambda i: (0, i, 0)),
        ]
        + [ANY] * len(kv_blocks),
        out_specs=[pl.BlockSpec((size, HD), lambda i: (i, 0))] + [VMEM] * 4 + [FAR] * 4,
        out_shape=[jax.ShapeDtypeStruct((BLOCK, HD), f32)]
        + [jax.ShapeDtypeStruct((2 * BLOCK, HD), bf16)] * 4
        + [pltpu.HBM((2 * BLOCK, HD), bf16)] * 4,
        scratch_shapes=KEYS + [pltpu.SemaphoreType.DMA((16,))] + [pltpu.VMEM((8 * BLOCK, HD), f32)] * 2,
        compiler_params=pltpu.CompilerParams(vmem_limit_bytes=32 << 20),
        cost_estimate=pl.CostEstimate(
            flops=8 * BLOCK * NSEL * BS * HD, bytes_accessed=15 << 20, transcendentals=0
        ),
        name="student_backward",
    )(meta, sel, queries, far(weights), grad_pieces, *kv_blocks)


def project(where, attn, weights, width, extra=None, after=()):
    composed = len(weights) == 1

    def pair(step, at):
        return step * 2 + at[0]

    if composed:
        w_specs = [pl.BlockSpec((8, 2, COUNTS, 3 * HD), lambda p, c: (0, pair(p, c), 0, 0))]
    else:
        w_specs = [
            pl.BlockSpec((HD, 2 * width), lambda p, c: (0, pair(p, c))),
            pl.BlockSpec((2 * HD, 2 * width), lambda p, c: (0, pair(p, c))),
        ]
    out_spec = pl.BlockSpec((2, BLOCK, width), lambda p, c: (p, 0, 0))
    more = [] if extra is None else [extra]
    args = [far(a) for a in attn] + list(weights) + more + list(after)

    def kernel(at, s_ref, a_ref, b_ref, *refs):
        first = pl.multiple_of(at[1] * HD, HD)
        second = pl.multiple_of((1 - at[1]) * HD, HD)

        def store(k, acc):
            if extra is not None:
                acc = acc + refs[len(weights)][k].astype(f32)
            refs[-1][k] = acc.astype(bf16)

        if composed:
            here, back = a_ref[...], b_ref[...]
            low = jnp.where(at[1] == 0, here, back)
            high = jnp.where(at[1] == 0, back, here)
            for k in range(2):
                wide = refs[0][:, k].reshape(HD, 3 * HD)

                def times(value, j):
                    return lax.dot_general(
                        value, wide[:, j * HD : (j + 1) * HD], ROWS_NT, preferred_element_type=f32
                    )

                store(k, times(s_ref[...], 0) - times(low, 1) - times(high, 2))
        else:
            for k in range(2):
                span = pl.ds(k * width, width)
                acc = jnp.dot(s_ref[...], refs[0][:, span], preferred_element_type=f32)
                for ref, start in ((a_ref, first), (b_ref, second)):
                    acc -= jnp.dot(
                        ref[...], refs[1][pl.ds(start, HD), span], preferred_element_type=f32
                    )
                store(k, acc)

    return pl.pallas_call(
        kernel,
        grid_spec=pltpu.PrefetchScalarGridSpec(
            num_scalar_prefetch=1,
            grid=(4,),
            in_specs=[pl.BlockSpec((BLOCK, HD), lambda p, c: (0, 0))] * 3
            + w_specs
            + [out_spec] * len(more)
            + [ANY] * len(after),
            out_specs=out_spec,
        ),
        out_shape=(pltpu.HBM if more else jax.ShapeDtypeStruct)((8, BLOCK, width), bf16),
        compiler_params=pltpu.CompilerParams(vmem_limit_bytes=20 << 20),
        cost_estimate=pl.CostEstimate(
            flops=2 * 8 * BLOCK * width * 3 * HD,
            bytes_accessed=2 * 8 * BLOCK * width * (1 + len(more)) + (2 << 20),
            transcendentals=0,
        ),
        name="project_grad" if composed else "project_mismatch",
    )(where, *args)


def token(*arrays):
    total = None
    for array in arrays:
        corner = array[:COUNTS, :] if array.ndim == 2 else array[0, :COUNTS, :]
        total = corner if total is None else total + corner
    return total


def gate(values, after):
    def kernel(*refs):
        pass

    n = len(values)
    return tuple(
        pl.pallas_call(
            kernel,
            in_specs=[FAR] * n + [ANY] * len(after),
            out_specs=[FAR] * n,
            out_shape=[pltpu.HBM(v.shape, v.dtype) for v in values],
            input_output_aliases={k: k for k in range(n)},
            name="gate",
        )(*map(far, values), *after)
    )


def pack_kernel(at, seg_ref, tq_ref, tk_ref, tv_ref, sk_ref, sv_ref, so_ref, *refs):
    outs, stages, sems = refs[:5], refs[5:10], refs[10]
    s_own, t_sent, rows, q_own, t_own = stages
    near = pl.ds(pl.multiple_of(at[0] * HD, HD), HD)
    other = pl.ds(pl.multiple_of((1 - at[0]) * HD, HD), HD)
    started = 0

    def move(source, target):
        nonlocal started
        copy = pltpu.make_async_copy(source, target, sems.at[started])
        copy.start()
        started += 1
        return copy

    keys, values, last = pl.ds(0, BLOCK), pl.ds(BLOCK, BLOCK), pl.ds(2 * BLOCK, COUNTS)
    part = pl.ds(pl.multiple_of(at[1] * COUNTS, COUNTS), COUNTS)
    more = pl.ds(SPAN, BLOCK)
    coming = (
        (0, [move(sk_ref, s_own.at[keys]), move(sv_ref, s_own.at[values])]),
        (
            1,
            [
                move(tk_ref.at[:, other], t_sent.at[keys]),
                move(tv_ref.at[:, other], t_sent.at[values]),
                move(tq_ref.at[:, other], t_sent.at[more]),
            ],
        ),
        (2, [move(so_ref.at[part], rows)]),
        (4, [move(tk_ref.at[:, near], t_own.at[keys]), move(tv_ref.at[:, near], t_own.at[values])]),
        (3, [move(tq_ref.at[:, near], q_own)]),
    )
    found = jnp.sum((seg_ref[...] == 0).astype(f32), axis=0, keepdims=True)
    first = lax.broadcasted_iota(jnp.int32, (COUNTS, HD), 0) == 0
    counts = jnp.where(first, found, 0.0).astype(bf16)
    for stage in (s_own, t_own, t_sent):
        stage[last, :] = counts
    going = []
    for k, copies in coming:
        for copy in copies:
            copy.wait()
        going.append(move(stages[k], outs[k]))
    for copy in going:
        copy.wait()


def pack(at, seg, *arrays):
    short = (BLOCK, HD)
    span = (SPAN, HD)
    shapes = [span, (SPAN + BLOCK, HD), (COUNTS, arrays[-1].shape[1]), short, span]
    return pl.pallas_call(
        pack_kernel,
        in_specs=[pl.BlockSpec(memory_space=SMEM), VMEM] + [FAR] * 6,
        out_specs=[FAR] * 5,
        out_shape=[pltpu.HBM(shape, bf16) for shape in shapes],
        scratch_shapes=[pltpu.VMEM(shape, bf16) for shape in shapes] + [pltpu.SemaphoreType.DMA((14,))],
        compiler_params=pltpu.CompilerParams(vmem_limit_bytes=12 << 20),
        cost_estimate=pl.CostEstimate(flops=0, bytes_accessed=5 << 20, transcendentals=0),
        name="pack",
    )(at, seg, *map(far, arrays))


def repack_kernel(kept_ref, *refs):
    target, sem = refs[-3], refs[-1]
    copy = pltpu.make_async_copy(kept_ref, target.at[pl.ds(0, SPAN)], sem)
    copy.start()
    target[SPAN:, :] = refs[0][:SPAN, :]
    for k, ref in enumerate(refs[1:4]):
        refs[-2][k * SPAN : (k + 1) * SPAN, :] = ref[...]
    copy.wait()


def repack(kept, got, student, after):
    return pl.pallas_call(
        repack_kernel,
        in_specs=[FAR] + [VMEM] * 4 + [ANY] * len(after),
        out_specs=[VMEM] * 2,
        out_shape=[jax.ShapeDtypeStruct((k * SPAN, HD), bf16) for k in (2, 3)],
        scratch_shapes=[pltpu.SemaphoreType.DMA],
        compiler_params=pltpu.CompilerParams(vmem_limit_bytes=8 << 20),
        cost_estimate=pl.CostEstimate(flops=0, bytes_accessed=5 << 20, transcendentals=0),
        name="repack",
    )(far(kept), got, *student, *after)


def compose_kernel(rows_ref, s_ref, t_ref, *refs):
    out_ref, acc = refs[-2:]
    step = pl.program_id(0)

    @pl.when(step == 0)
    def _():
        acc[...] = jnp.zeros_like(acc)

    rows = rows_ref[...]
    for ref, low, high in ((s_ref, 0, HD), (t_ref, HD, 3 * HD)):
        acc[:, low:high] += lax.dot_general(rows, ref[...], ROWS_NT, preferred_element_type=f32)

    @pl.when(step == pl.num_programs(0) - 1)
    def _():
        out_ref[...] = acc[...].astype(bf16)


def compose(rows, s_out, t_out, after):
    count, depth = rows.shape
    size = depth // 4
    return pl.pallas_call(
        compose_kernel,
        grid=(4,),
        in_specs=[pl.BlockSpec((n, size), lambda i: (0, i)) for n in (count, HD, 2 * HD)]
        + [ANY] * len(after),
        out_specs=pl.BlockSpec((count, 3 * HD), lambda i: (0, 0)),
        out_shape=pltpu.HBM((count, 3 * HD), bf16),
        scratch_shapes=[pltpu.VMEM((count, 3 * HD), f32)],
        compiler_params=pltpu.CompilerParams(vmem_limit_bytes=12 << 20),
        cost_estimate=pl.CostEstimate(
            flops=2 * count * 3 * HD * depth, bytes_accessed=5 << 20, transcendentals=0
        ),
        name="compose",
    )(far(rows), s_out, t_out, *after)


def add_pieces_kernel(in_ref, out_ref):
    out_ref[...] = jnp.sum(in_ref[...].astype(f32), axis=0)


def add_pieces(pieces):
    count, rows, width = pieces.shape
    size = rows // 4
    return pl.pallas_call(
        add_pieces_kernel,
        grid=(4,),
        in_specs=[pl.BlockSpec((count, size, width), lambda i: (0, i, 0))],
        out_specs=pl.BlockSpec((size, width), lambda i: (i, 0)),
        out_shape=jax.ShapeDtypeStruct((rows, width), f32),
        compiler_params=pltpu.CompilerParams(vmem_limit_bytes=16 << 20),
        cost_estimate=pl.CostEstimate(flops=8 << 20, bytes_accessed=5 << 20, transcendentals=0),
        name="add_pieces",
    )(pieces)


def finish_kernel(at, *refs):
    low, across, high, (dk_ref, dv_ref) = refs[:4], refs[4], refs[5:9], refs[-2:]

    def write(parts):
        for ref, span in ((dk_ref, pl.ds(0, BLOCK)), (dv_ref, pl.ds(BLOCK, BLOCK))):
            total = parts[0][span, :].astype(f32)
            for part in parts[1:]:
                total = total + part[span, :].astype(f32)
            ref[...] = total

    @pl.when(at[0] == 0)
    def _():
        write(low + (across,))

    @pl.when(at[0] == 1)
    def _():
        write(high)


def finish(at, low, across, high, after):
    near = [pltpu.with_memory_space_constraint(part, pltpu.VMEM) for part in (*low, across, *high)]
    return pl.pallas_call(
        finish_kernel,
        in_specs=[pl.BlockSpec(memory_space=SMEM)] + [VMEM] * 9 + [ANY] * len(after),
        out_specs=[pl.BlockSpec((BLOCK, HD), lambda: (0, 0))] * 2,
        out_shape=[pltpu.HBM((BLOCK, HD), f32)] * 2,
        compiler_params=pltpu.CompilerParams(vmem_limit_bytes=16 << 20),
        cost_estimate=pl.CostEstimate(flops=4 << 20, bytes_accessed=5 << 20, transcendentals=0),
        name="finish",
    )(at, *near, *after)


def on_device(t_query, t_key, t_value, t_out, s_query, s_key, s_value, s_out, segments, selection):
    x, y, core = lax.axis_index("xlo"), lax.axis_index("y"), lax.axis_index("core")
    mine = 4 * x + y
    partner = 4 * (1 - x) + y

    def along_y(block, all_x, causal_x):
        return tuple(
            lax.ppermute(block, BLK, y_pairs(shift, all_x, causal_x)) for shift in (1, -1, 2)
        )

    to_partner = [(i, i ^ 4) for i in range(8)]
    at_x = jnp.stack([x, mine]).astype(jnp.int32)
    s_own, t_sent, rows, q_own, t_own = pack(
        at_x, segments.reshape(8, HD), t_query, t_key, t_value, s_key, s_value, s_out
    )
    up = [(i, i + 4) for i in range(4)]
    s_near = along_y(s_own, (0,), (1,))
    t_got = lax.ppermute(t_sent, BLK, to_partner)
    s_low = lax.ppermute(s_own, BLK, up)
    t_two, s_three = repack(t_own, t_got, s_near, (token(s_low),))
    t_near = along_y(t_two, (0, 1), ())
    s_lows = lax.ppermute(s_three, BLK, up)

    def place_of(block):
        step = (block + 4 - y) % 4
        return jnp.where(step == 0, 0, jnp.where(step == 3, 1, step + 1)), (block // 4 != x).astype(jnp.int32)

    spot, half = place_of(jnp.arange(8, dtype=jnp.int32))
    t_meta = jnp.concatenate([jnp.stack([mine, partner] + [0] * 6).astype(jnp.int32), 2 * spot + half])
    spot, half = place_of(selection // 16)
    sel = ((spot + 4 * half) * BLOCK + selection % 16 * BS).reshape(-1).astype(jnp.int32)
    k_pos = (selection[:, :, None] * BS + jnp.arange(BS, dtype=jnp.int32)).reshape(-1, 1, NSEL * BS)
    s_meta = jnp.stack([mine, x]).astype(jnp.int32)

    s_blocks = tuple(map(far, (s_own, *s_near, s_low, s_lows)))
    s_attn, weights = student_forward(s_meta, sel, s_query, k_pos, s_blocks)

    rows = lax.all_gather(rows, GROUP, axis=0, tiled=True)
    through = compose(rows, s_out, t_out, (token(*t_near, s_attn),))
    through = lax.all_gather(through, BLK, axis=0, tiled=True).reshape(8, 16, HD // 8, 3 * HD)

    t_blocks = tuple(map(far, (t_own, t_got, *t_near)))
    away, here = teacher_attention(t_meta, q_own, t_blocks)
    back = lax.ppermute(away, BLK, to_partner)
    attn = (s_attn, here, back)

    this = jnp.stack([core, x]).astype(jnp.int32)
    other = jnp.stack([1 - core, x]).astype(jnp.int32)
    to_core = [(0, 1), (1, 0)]
    part = project(other, attn, (s_out, t_out), 2 * HD)
    grad = project(other, attn, (through,), HD, None, (token(part),))
    grad = lax.ppermute(grad, "core", to_core)
    grad = project(this, attn, (through,), HD, grad)
    grad = lax.all_to_all(grad, ZX, 0, 0, tiled=True)
    part = lax.ppermute(part, "core", to_core)
    part = project(this, attn, (s_out, t_out), 2 * HD, part)
    part = lax.all_to_all(part, ZX, 0, 0, tiled=True)

    out = student_backward(s_meta, sel, s_query, weights, grad, s_blocks)
    s_dq, pieces = out[0], out[1:]

    def earlier(shift, all_x, causal_x):
        pairs = []
        for i in range(2):
            for j in range(4):
                to = (j + shift) % 4
                if i in all_x or (i in causal_x and to < j):
                    pairs.append((4 * i + j, 4 * i + to))
        return pairs

    low, high = list(pieces[:4]), list(pieces[4:])
    for j, shift in ((1, -1), (2, 1), (3, 2)):
        low[j] = lax.ppermute(low[j], BLK, earlier(shift, (1,), (0,)))
    low_sum = low[0].astype(f32) + low[1].astype(f32) + low[2].astype(f32) + low[3].astype(f32)
    across = low_sum.astype(bf16)
    high = list(gate(high, (token(across),)))
    across = lax.ppermute(across, BLK, [(i + 4, i) for i in range(4)])
    for j, shift in ((1, -1), (2, 1), (3, 2)):
        high[j] = lax.ppermute(high[j], BLK, earlier(shift, (), (1,)))
    mismatch = add_pieces(part)
    s_dk, s_dv = finish(at_x, tuple(low), across, tuple(high), (token(mismatch[:, :HD]),))
    return mismatch, s_dq, s_dk, s_dv


def solution(mesh):
    fine = Mesh(mesh.devices.reshape(2, 4, 4, 2, 2), ("xlo", "y", "z", "core", "xhi"))
    data = P(BLK, GROUP)
    flat = P(GROUP, None)
    return jax.shard_map(
        on_device,
        mesh=fine,
        in_specs=(data, data, data, flat, data, data, data, flat, P(BLK), P(BLK, None)),
        out_specs=(data, data, data, data),
        check_vma=False,
    )
```

```python
import jax
import jax.numpy as jnp
from jax import lax
from jax.experimental import pallas as pl
from jax.experimental.pallas import tpu as pltpu
from jax.sharding import Mesh
from jax.sharding import PartitionSpec as P

HD = 128
BS = 64
NSEL = 16
BLOCK = 1024
COUNTS = 16
FORWARD_ROWS = 4
BACKWARD_ROWS = 4
TILE_Q = 512
TILE_K = 1024
SCALE = HD ** (-0.5)
EXP_SCALE = SCALE * 1.4426950408889634
LOWEST = -1e30

BLK = ("xlo", "y")
GROUP = ("z", "core", "xhi")
ZX = ("z", "xhi")
f32 = jnp.float32
bf16 = jnp.bfloat16

SMEM = pltpu.SMEM
ANY = pl.BlockSpec(memory_space=pl.ANY)
FAR = pl.BlockSpec(memory_space=pltpu.HBM)

VMEM = pl.BlockSpec(memory_space=pltpu.VMEM)
ROWS_NT = (((1,), (1,)), ((), ()))
ROWS_TN = (((0,), (0,)), ((), ()))


def y_pairs(shift, all_x, causal_x):
    pairs = []
    for x in range(2):
        for y in range(4):
            to = (y + shift) % 4
            if x in all_x or (x in causal_x and y < to):
                pairs.append((4 * x + y, 4 * x + to))
    return pairs


def far(array):
    return pltpu.with_memory_space_constraint(array, pltpu.HBM)


SPAN = 2 * BLOCK + COUNTS


def blocks_of(refs):
    return [(ref, k * SPAN) for ref in refs for k in range(ref.shape[0] // SPAN)]


def load(blocks, key_all, value_all, counts, sems, meanwhile=None):
    copies = []

    def bring(source, target):
        copy = pltpu.make_async_copy(source, target, sems.at[len(copies)])
        copy.start()
        copies.append(copy)

    for j, (ref, at) in enumerate(blocks):
        slot = pl.ds(j * BLOCK, BLOCK)
        bring(ref.at[pl.ds(at, BLOCK)], key_all.at[slot])
        bring(ref.at[pl.ds(at + BLOCK, BLOCK)], value_all.at[slot])
        if counts is not None:
            bring(ref.at[pl.ds(at + 2 * BLOCK, COUNTS)], counts.at[pl.ds(j * COUNTS, COUNTS)])
    if meanwhile is not None:
        meanwhile()
    for copy in copies:
        copy.wait()


def border_of(counts):
    return jnp.sum(counts[...].astype(f32)).astype(jnp.int32)


KEYS = [pltpu.VMEM((8 * BLOCK, HD), bf16)] * 2
WITH_COUNTS = KEYS + [pltpu.VMEM((8 * COUNTS, HD), bf16), pltpu.SemaphoreType.DMA((24,))]


def teacher_kernel(meta, here_ref, *refs):
    blocks = blocks_of(refs[:-8])
    away_out, here_out, key_all, value_all, counts, sems, away_ref, away_sem = refs[-8:]
    away_copy = pltpu.make_async_copy(refs[1].at[pl.ds(SPAN, BLOCK)], away_ref, away_sem)
    away_copy.start()
    load(blocks, key_all, value_all, counts, sems)
    away_copy.wait()
    border = border_of(counts)
    per_block = BLOCK // TILE_K

    def one_block(q_ref, o_ref, block):
        first = block * BLOCK
        tiles = []
        for step in range(BLOCK // TILE_Q):
            q_pos = first + step * TILE_Q + lax.broadcasted_iota(jnp.int32, (TILE_Q, 1), 0)
            q_low = jnp.where(q_pos >= border, border, 0)
            tiles.append((q_ref[pl.ds(step * TILE_Q, TILE_Q), :], q_pos, q_low))

        def turn(masked, j, tile, carry):
            queries, q_pos, q_low = tile
            largest, total, acc = carry
            slot = meta[8 + j // per_block]
            start = pl.multiple_of(slot * BLOCK + (j % per_block) * TILE_K, TILE_K)
            scores = lax.dot_general(
                queries, key_all[pl.ds(start, TILE_K), :], ROWS_NT, preferred_element_type=f32
            )
            if masked:
                k_pos = j * TILE_K + lax.broadcasted_iota(jnp.int32, (1, TILE_K), 1)
                scores = jnp.where((k_pos <= q_pos) & (k_pos >= q_low), scores, LOWEST)
            new = jnp.maximum(largest, jnp.max(scores, axis=1, keepdims=True))
            factor = jnp.exp2((largest - new) * EXP_SCALE)
            weights = jnp.exp2((scores - new) * EXP_SCALE)
            total = factor * total + jnp.sum(weights, axis=1, keepdims=True)
            acc = factor * acc + jnp.dot(
                weights.astype(bf16), value_all[pl.ds(start, TILE_K), :], preferred_element_type=f32
            )
            return new, total, acc

        def turns(masked, j, carries):
            return tuple(turn(masked, j, tile, carry) for tile, carry in zip(tiles, carries))

        carries = tuple(
            (
                jnp.full((TILE_Q, 1), LOWEST, f32),
                jnp.zeros((TILE_Q, 1), f32),
                jnp.zeros((TILE_Q, HD), f32),
            )
            for _ in tiles
        )
        begin = jnp.where(first >= border, border, 0) // TILE_K
        diagonal = first // TILE_K
        low_last = jnp.where(first + BLOCK - 1 >= border, border, 0)
        clear = jnp.minimum((low_last + TILE_K - 1) // TILE_K, diagonal)
        carries = lax.fori_loop(begin, clear, lambda j, c: turns(True, j, c), carries)
        carries = lax.fori_loop(clear, diagonal, lambda j, c: turns(False, j, c), carries)
        carries = list(carries)
        for k in range(per_block):
            for n, tile in enumerate(tiles):
                if k * TILE_K < (n + 1) * TILE_Q:
                    carries[n] = turn(True, diagonal + k, tile, carries[n])
        for step, (_, total, acc) in enumerate(carries):
            o_ref[pl.ds(step * TILE_Q, TILE_Q), :] = (acc / total).astype(bf16)

    one_block(away_ref, away_out, meta[1])
    one_block(here_ref, here_out, meta[0])


def teacher_attention(meta, here, kv_blocks):
    return pl.pallas_call(
        teacher_kernel,
        in_specs=[pl.BlockSpec(memory_space=SMEM), pl.BlockSpec((BLOCK, HD), lambda: (0, 0))]
        + [ANY] * len(kv_blocks),
        out_specs=[pl.BlockSpec((BLOCK, HD), lambda: (0, 0))] * 2,
        out_shape=[pltpu.HBM((BLOCK, HD), bf16)] * 2,
        scratch_shapes=WITH_COUNTS + [pltpu.VMEM((BLOCK, HD), bf16), pltpu.SemaphoreType.DMA],
        compiler_params=pltpu.CompilerParams(vmem_limit_bytes=24 << 20),
        cost_estimate=pl.CostEstimate(
            flops=8 * 4 * BLOCK * BLOCK * HD, bytes_accessed=5 << 20, transcendentals=8 * BLOCK * BLOCK
        ),
        name="teacher_attention",
    )(meta, far(here), *kv_blocks)


def chosen_rows(sel, row, table):
    pieces = []
    for n in range(NSEL):
        start = pl.multiple_of(sel[row * NSEL + n], BS)
        pieces.append(table[pl.ds(start, BS), :])
    return jnp.concatenate(pieces, axis=0)


def student_forward_kernel(meta, sel, q_ref, kpos_ref, *refs):
    blocks = blocks_of(refs[:-6])
    o_ref, p_ref, key_all, value_all, counts, sems = refs[-6:]
    step = pl.program_id(0)

    @pl.when(step == 0)
    def _():
        load(blocks, key_all, value_all, counts, sems)

    border = border_of(counts)
    for u in range(FORWARD_ROWS):
        row = step * FORWARD_ROWS + u
        span = pl.ds(u * BS, BS)
        q_pos = meta[0] * BLOCK + row * BS + lax.broadcasted_iota(jnp.int32, (BS, 1), 0)
        q_low = jnp.where(q_pos >= border, border, 0)
        k_pos = kpos_ref[u]
        scores = lax.dot_general(
            q_ref[span, :], chosen_rows(sel, row, key_all), ROWS_NT, preferred_element_type=f32
        )
        scores = jnp.where((k_pos <= q_pos) & (k_pos >= q_low), scores, LOWEST)
        weights = jnp.exp2((scores - jnp.max(scores, axis=1, keepdims=True)) * EXP_SCALE)
        inverse = 1.0 / jnp.sum(weights, axis=1, keepdims=True)
        p_ref[span, :] = weights * inverse
        blended = jnp.dot(
            weights.astype(bf16), chosen_rows(sel, row, value_all), preferred_element_type=f32
        )
        o_ref[span, :] = (blended * inverse).astype(bf16)


def student_forward(meta, sel, queries, k_pos, kv_blocks):
    size = FORWARD_ROWS * BS
    return pl.pallas_call(
        student_forward_kernel,
        grid=(BLOCK // size,),
        in_specs=[
            pl.BlockSpec(memory_space=SMEM),
            pl.BlockSpec(memory_space=SMEM),
            pl.BlockSpec((size, HD), lambda i: (i, 0)),
            pl.BlockSpec((FORWARD_ROWS, 1, NSEL * BS), lambda i: (i, 0, 0)),
        ]
        + [ANY] * len(kv_blocks),
        out_specs=[
            pl.BlockSpec((size, HD), lambda i: (i, 0)),
            pl.BlockSpec((size, NSEL * BS), lambda i: (i, 0)),
        ],
        out_shape=[
            pltpu.HBM((BLOCK, HD), bf16),
            pltpu.HBM((BLOCK, NSEL * BS), f32),
        ],
        scratch_shapes=WITH_COUNTS,
        compiler_params=pltpu.CompilerParams(vmem_limit_bytes=24 << 20),
        cost_estimate=pl.CostEstimate(
            flops=4 * BLOCK * NSEL * BS * HD, bytes_accessed=9 << 20, transcendentals=BLOCK * NSEL * BS
        ),
        name="student_forward",
    )(meta, sel, queries, k_pos, *kv_blocks)


def student_backward_kernel(meta, sel, q_ref, p_ref, g_ref, *refs):
    blocks = blocks_of(refs[:-14])
    dq_ref, out_refs = refs[-14], refs[-13:-5]
    key_all, value_all, sems, dk_all, dv_all = refs[-5:]
    step = pl.program_id(0)

    @pl.when(step == 0)
    def _():
        def clear():
            dk_all[...] = jnp.zeros_like(dk_all)
            dv_all[...] = jnp.zeros_like(dv_all)

        load(blocks, key_all, value_all, None, sems, clear)

    for u in range(BACKWARD_ROWS):
        row = step * BACKWARD_ROWS + u
        span = pl.ds(u * BS, BS)
        grad = jnp.sum(g_ref[:, span, :].astype(f32), axis=0).astype(bf16)
        weights = p_ref[span, :]
        weight_grad = lax.dot_general(
            grad, chosen_rows(sel, row, value_all), ROWS_NT, preferred_element_type=f32
        )
        row_dots = jnp.sum(weights * weight_grad, axis=1, keepdims=True)
        score_grad = (weights * (weight_grad - row_dots) * SCALE).astype(bf16)
        dq_ref[span, :] = jnp.dot(
            score_grad, chosen_rows(sel, row, key_all), preferred_element_type=f32
        )
        key_grad = lax.dot_general(score_grad, q_ref[span, :], ROWS_TN, preferred_element_type=f32)
        value_grad = lax.dot_general(
            weights.astype(bf16), grad, ROWS_TN, preferred_element_type=f32
        )
        for n in range(NSEL):
            start = pl.multiple_of(sel[row * NSEL + n], BS)
            dk_all[pl.ds(start, BS), :] += key_grad[n * BS : (n + 1) * BS, :]
            dv_all[pl.ds(start, BS), :] += value_grad[n * BS : (n + 1) * BS, :]

    @pl.when(step == pl.num_programs(0) - 1)
    def _():
        copies = []
        for j in (4, 5, 6, 7, 0, 1, 2, 3):
            ref = out_refs[j]
            start = pl.multiple_of((meta[1] * 4 + j) % 8 * BLOCK, BLOCK)
            for k, (total, table) in enumerate(((dk_all, key_all), (dv_all, value_all))):
                spot = pl.ds(k * BLOCK, BLOCK)
                if j < 4:
                    ref[spot, :] = total[pl.ds(start, BLOCK), :].astype(bf16)
                    continue
                slot = pl.ds((j - 4) * BLOCK, BLOCK)
                table[slot, :] = total[pl.ds(start, BLOCK), :].astype(bf16)
                copy = pltpu.make_async_copy(table.at[slot], ref.at[spot], sems.at[len(copies)])
                copy.start()
                copies.append(copy)
        for copy in copies:
            copy.wait()


def student_backward(meta, sel, queries, weights, grad_pieces, kv_blocks):
    size = BACKWARD_ROWS * BS
    return pl.pallas_call(
        student_backward_kernel,
        grid=(BLOCK // size,),
        in_specs=[
            pl.BlockSpec(memory_space=SMEM),
            pl.BlockSpec(memory_space=SMEM),
            pl.BlockSpec((size, HD), lambda i: (i, 0)),
            pl.BlockSpec((size, NSEL * BS), lambda i: (i, 0)),
            pl.BlockSpec((8, size, HD), lambda i: (0, i, 0)),
        ]
        + [ANY] * len(kv_blocks),
        out_specs=[pl.BlockSpec((size, HD), lambda i: (i, 0))] + [VMEM] * 4 + [FAR] * 4,
        out_shape=[jax.ShapeDtypeStruct((BLOCK, HD), f32)]
        + [jax.ShapeDtypeStruct((2 * BLOCK, HD), bf16)] * 4
        + [pltpu.HBM((2 * BLOCK, HD), bf16)] * 4,
        scratch_shapes=KEYS + [pltpu.SemaphoreType.DMA((16,))] + [pltpu.VMEM((8 * BLOCK, HD), f32)] * 2,
        compiler_params=pltpu.CompilerParams(vmem_limit_bytes=32 << 20),
        cost_estimate=pl.CostEstimate(
            flops=8 * BLOCK * NSEL * BS * HD, bytes_accessed=15 << 20, transcendentals=0
        ),
        name="student_backward",
    )(meta, sel, queries, far(weights), grad_pieces, *kv_blocks)


def project(where, attn, weights, width, extra=None, after=()):
    composed = len(weights) == 1

    def pair(step, at):
        return step * 2 + at[0]

    if composed:
        w_specs = [pl.BlockSpec((8, 2, COUNTS, 3 * HD), lambda p, c: (0, pair(p, c), 0, 0))]
    else:
        w_specs = [
            pl.BlockSpec((HD, 2 * width), lambda p, c: (0, pair(p, c))),
            pl.BlockSpec((2 * HD, 2 * width), lambda p, c: (0, pair(p, c))),
        ]
    out_spec = pl.BlockSpec((2, BLOCK, width), lambda p, c: (p, 0, 0))
    more = [] if extra is None else [extra]
    args = [far(a) for a in attn] + list(weights) + more + list(after)

    def kernel(at, s_ref, a_ref, b_ref, *refs):
        first = pl.multiple_of(at[1] * HD, HD)
        second = pl.multiple_of((1 - at[1]) * HD, HD)

        def store(k, acc):
            if extra is not None:
                acc = acc + refs[len(weights)][k].astype(f32)
            refs[-1][k] = acc.astype(bf16)

        if composed:
            here, back = a_ref[...], b_ref[...]
            low = jnp.where(at[1] == 0, here, back)
            high = jnp.where(at[1] == 0, back, here)
            for k in range(2):
                wide = refs[0][:, k].reshape(HD, 3 * HD)

                def times(value, j):
                    return lax.dot_general(
                        value, wide[:, j * HD : (j + 1) * HD], ROWS_NT, preferred_element_type=f32
                    )

                store(k, times(s_ref[...], 0) - times(low, 1) - times(high, 2))
        else:
            for k in range(2):
                span = pl.ds(k * width, width)
                acc = jnp.dot(s_ref[...], refs[0][:, span], preferred_element_type=f32)
                for ref, start in ((a_ref, first), (b_ref, second)):
                    acc -= jnp.dot(
                        ref[...], refs[1][pl.ds(start, HD), span], preferred_element_type=f32
                    )
                store(k, acc)

    return pl.pallas_call(
        kernel,
        grid_spec=pltpu.PrefetchScalarGridSpec(
            num_scalar_prefetch=1,
            grid=(4,),
            in_specs=[pl.BlockSpec((BLOCK, HD), lambda p, c: (0, 0))] * 3
            + w_specs
            + [out_spec] * len(more)
            + [ANY] * len(after),
            out_specs=out_spec,
        ),
        out_shape=(pltpu.HBM if more else jax.ShapeDtypeStruct)((8, BLOCK, width), bf16),
        compiler_params=pltpu.CompilerParams(vmem_limit_bytes=20 << 20),
        cost_estimate=pl.CostEstimate(
            flops=2 * 8 * BLOCK * width * 3 * HD,
            bytes_accessed=2 * 8 * BLOCK * width * (1 + len(more)) + (2 << 20),
            transcendentals=0,
        ),
        name="project_grad" if composed else "project_mismatch",
    )(where, *args)


def token(*arrays):
    total = None
    for array in arrays:
        corner = array[:COUNTS, :] if array.ndim == 2 else array[0, :COUNTS, :]
        total = corner if total is None else total + corner
    return total


def gate(values, after):
    def kernel(*refs):
        pass

    n = len(values)
    return tuple(
        pl.pallas_call(
            kernel,
            in_specs=[FAR] * n + [ANY] * len(after),
            out_specs=[FAR] * n,
            out_shape=[pltpu.HBM(v.shape, v.dtype) for v in values],
            input_output_aliases={k: k for k in range(n)},
            name="gate",
        )(*map(far, values), *after)
    )


def pack_kernel(at, seg_ref, tq_ref, tk_ref, tv_ref, sk_ref, sv_ref, so_ref, *refs):
    outs, stages, sems = refs[:5], refs[5:10], refs[10]
    s_own, t_sent, rows, q_own, t_own = stages
    near = pl.ds(pl.multiple_of(at[0] * HD, HD), HD)
    other = pl.ds(pl.multiple_of((1 - at[0]) * HD, HD), HD)
    started = 0

    def move(source, target):
        nonlocal started
        copy = pltpu.make_async_copy(source, target, sems.at[started])
        copy.start()
        started += 1
        return copy

    keys, values, last = pl.ds(0, BLOCK), pl.ds(BLOCK, BLOCK), pl.ds(2 * BLOCK, COUNTS)
    part = pl.ds(pl.multiple_of(at[1] * COUNTS, COUNTS), COUNTS)
    more = pl.ds(SPAN, BLOCK)
    coming = (
        (0, [move(sk_ref, s_own.at[keys]), move(sv_ref, s_own.at[values])]),
        (
            1,
            [
                move(tk_ref.at[:, other], t_sent.at[keys]),
                move(tv_ref.at[:, other], t_sent.at[values]),
                move(tq_ref.at[:, other], t_sent.at[more]),
            ],
        ),
        (2, [move(so_ref.at[part], rows)]),
        (4, [move(tk_ref.at[:, near], t_own.at[keys]), move(tv_ref.at[:, near], t_own.at[values])]),
        (3, [move(tq_ref.at[:, near], q_own)]),
    )
    found = jnp.sum((seg_ref[...] == 0).astype(f32), axis=0, keepdims=True)
    first = lax.broadcasted_iota(jnp.int32, (COUNTS, HD), 0) == 0
    counts = jnp.where(first, found, 0.0).astype(bf16)
    for stage in (s_own, t_own, t_sent):
        stage[last, :] = counts
    going = []
    for k, copies in coming:
        for copy in copies:
            copy.wait()
        going.append(move(stages[k], outs[k]))
    for copy in going:
        copy.wait()


def pack(at, seg, *arrays):
    short = (BLOCK, HD)
    span = (SPAN, HD)
    shapes = [span, (SPAN + BLOCK, HD), (COUNTS, arrays[-1].shape[1]), short, span]
    return pl.pallas_call(
        pack_kernel,
        in_specs=[pl.BlockSpec(memory_space=SMEM), VMEM] + [FAR] * 6,
        out_specs=[FAR] * 5,
        out_shape=[pltpu.HBM(shape, bf16) for shape in shapes],
        scratch_shapes=[pltpu.VMEM(shape, bf16) for shape in shapes] + [pltpu.SemaphoreType.DMA((14,))],
        compiler_params=pltpu.CompilerParams(vmem_limit_bytes=12 << 20),
        cost_estimate=pl.CostEstimate(flops=0, bytes_accessed=5 << 20, transcendentals=0),
        name="pack",
    )(at, seg, *map(far, arrays))


def repack_kernel(kept_ref, *refs):
    target, sem = refs[-3], refs[-1]
    copy = pltpu.make_async_copy(kept_ref, target.at[pl.ds(0, SPAN)], sem)
    copy.start()
    target[SPAN:, :] = refs[0][:SPAN, :]
    for k, ref in enumerate(refs[1:4]):
        refs[-2][k * SPAN : (k + 1) * SPAN, :] = ref[...]
    copy.wait()


def repack(kept, got, student, after):
    return pl.pallas_call(
        repack_kernel,
        in_specs=[FAR] + [VMEM] * 4 + [ANY] * len(after),
        out_specs=[VMEM] * 2,
        out_shape=[jax.ShapeDtypeStruct((k * SPAN, HD), bf16) for k in (2, 3)],
        scratch_shapes=[pltpu.SemaphoreType.DMA],
        compiler_params=pltpu.CompilerParams(vmem_limit_bytes=8 << 20),
        cost_estimate=pl.CostEstimate(flops=0, bytes_accessed=5 << 20, transcendentals=0),
        name="repack",
    )(far(kept), got, *student, *after)


def compose_kernel(rows_ref, s_ref, t_ref, *refs):
    out_ref, acc = refs[-2:]
    step = pl.program_id(0)

    @pl.when(step == 0)
    def _():
        acc[...] = jnp.zeros_like(acc)

    rows = rows_ref[...]
    for ref, low, high in ((s_ref, 0, HD), (t_ref, HD, 3 * HD)):
        acc[:, low:high] += lax.dot_general(rows, ref[...], ROWS_NT, preferred_element_type=f32)

    @pl.when(step == pl.num_programs(0) - 1)
    def _():
        out_ref[...] = acc[...].astype(bf16)


def compose(rows, s_out, t_out, after):
    count, depth = rows.shape
    size = depth // 4
    return pl.pallas_call(
        compose_kernel,
        grid=(4,),
        in_specs=[pl.BlockSpec((n, size), lambda i: (0, i)) for n in (count, HD, 2 * HD)]
        + [ANY] * len(after),
        out_specs=pl.BlockSpec((count, 3 * HD), lambda i: (0, 0)),
        out_shape=pltpu.HBM((count, 3 * HD), bf16),
        scratch_shapes=[pltpu.VMEM((count, 3 * HD), f32)],
        compiler_params=pltpu.CompilerParams(vmem_limit_bytes=12 << 20),
        cost_estimate=pl.CostEstimate(
            flops=2 * count * 3 * HD * depth, bytes_accessed=5 << 20, transcendentals=0
        ),
        name="compose",
    )(far(rows), s_out, t_out, *after)


def add_pieces_kernel(in_ref, out_ref):
    out_ref[...] = jnp.sum(in_ref[...].astype(f32), axis=0)


def add_pieces(pieces):
    count, rows, width = pieces.shape
    size = rows // 4
    return pl.pallas_call(
        add_pieces_kernel,
        grid=(4,),
        in_specs=[pl.BlockSpec((count, size, width), lambda i: (0, i, 0))],
        out_specs=pl.BlockSpec((size, width), lambda i: (i, 0)),
        out_shape=jax.ShapeDtypeStruct((rows, width), f32),
        compiler_params=pltpu.CompilerParams(vmem_limit_bytes=16 << 20),
        cost_estimate=pl.CostEstimate(flops=8 << 20, bytes_accessed=5 << 20, transcendentals=0),
        name="add_pieces",
    )(pieces)


def finish_kernel(at, *refs):
    low, across, high, (dk_ref, dv_ref) = refs[:4], refs[4], refs[5:9], refs[-2:]

    def write(parts):
        for ref, span in ((dk_ref, pl.ds(0, BLOCK)), (dv_ref, pl.ds(BLOCK, BLOCK))):
            total = parts[0][span, :].astype(f32)
            for part in parts[1:]:
                total = total + part[span, :].astype(f32)
            ref[...] = total

    @pl.when(at[0] == 0)
    def _():
        write(low + (across,))

    @pl.when(at[0] == 1)
    def _():
        write(high)


def finish(at, low, across, high, after):
    near = [pltpu.with_memory_space_constraint(part, pltpu.VMEM) for part in (*low, across, *high)]
    return pl.pallas_call(
        finish_kernel,
        in_specs=[pl.BlockSpec(memory_space=SMEM)] + [VMEM] * 9 + [ANY] * len(after),
        out_specs=[pl.BlockSpec((BLOCK, HD), lambda: (0, 0))] * 2,
        out_shape=[pltpu.HBM((BLOCK, HD), f32)] * 2,
        compiler_params=pltpu.CompilerParams(vmem_limit_bytes=16 << 20),
        cost_estimate=pl.CostEstimate(flops=4 << 20, bytes_accessed=5 << 20, transcendentals=0),
        name="finish",
    )(at, *near, *after)


def on_device(t_query, t_key, t_value, t_out, s_query, s_key, s_value, s_out, segments, selection):
    x, y, core = lax.axis_index("xlo"), lax.axis_index("y"), lax.axis_index("core")
    mine = 4 * x + y
    partner = 4 * (1 - x) + y

    def along_y(block, all_x, causal_x):
        return tuple(
            lax.ppermute(block, BLK, y_pairs(shift, all_x, causal_x)) for shift in (1, -1, 2)
        )

    to_partner = [(i, i ^ 4) for i in range(8)]
    at_x = jnp.stack([x, mine]).astype(jnp.int32)
    s_own, t_sent, rows, q_own, t_own = pack(
        at_x, segments.reshape(8, HD), t_query, t_key, t_value, s_key, s_value, s_out
    )
    up = [(i, i + 4) for i in range(4)]
    s_near = along_y(s_own, (0,), (1,))
    t_got = lax.ppermute(t_sent, BLK, to_partner)
    s_low = lax.ppermute(s_own, BLK, up)
    t_two, s_three = repack(t_own, t_got, s_near, (token(s_low),))
    t_near = along_y(t_two, (0, 1), ())
    s_lows = lax.ppermute(s_three, BLK, up)

    def place_of(block):
        step = (block + 4 - y) % 4
        return jnp.where(step == 0, 0, jnp.where(step == 3, 1, step + 1)), (block // 4 != x).astype(jnp.int32)

    spot, half = place_of(jnp.arange(8, dtype=jnp.int32))
    t_meta = jnp.concatenate([jnp.stack([mine, partner] + [0] * 6).astype(jnp.int32), 2 * spot + half])
    spot, half = place_of(selection // 16)
    sel = ((spot + 4 * half) * BLOCK + selection % 16 * BS).reshape(-1).astype(jnp.int32)
    k_pos = (selection[:, :, None] * BS + jnp.arange(BS, dtype=jnp.int32)).reshape(-1, 1, NSEL * BS)
    s_meta = jnp.stack([mine, x]).astype(jnp.int32)

    s_blocks = tuple(map(far, (s_own, *s_near, s_low, s_lows)))
    s_attn, weights = student_forward(s_meta, sel, s_query, k_pos, s_blocks)

    rows = lax.all_gather(rows, GROUP, axis=0, tiled=True)
    through = compose(rows, s_out, t_out, (token(*t_near, s_attn),))
    through = lax.all_gather(through, BLK, axis=0, tiled=True).reshape(8, 16, HD // 8, 3 * HD)

    t_blocks = tuple(map(far, (t_own, t_got, *t_near)))
    away, here = teacher_attention(t_meta, q_own, t_blocks)
    back = lax.ppermute(away, BLK, to_partner)
    attn = (s_attn, here, back)

    this = jnp.stack([core, x]).astype(jnp.int32)
    other = jnp.stack([1 - core, x]).astype(jnp.int32)
    to_core = [(0, 1), (1, 0)]
    part = project(other, attn, (s_out, t_out), 2 * HD)
    grad = project(other, attn, (through,), HD, None, (token(part),))
    grad = lax.ppermute(grad, "core", to_core)
    grad = project(this, attn, (through,), HD, grad)
    grad = lax.all_to_all(grad, ZX, 0, 0, tiled=True)
    part = lax.ppermute(part, "core", to_core)
    part = project(this, attn, (s_out, t_out), 2 * HD, part)
    part = lax.all_to_all(part, ZX, 0, 0, tiled=True)

    out = student_backward(s_meta, sel, s_query, weights, grad, s_blocks)
    s_dq, pieces = out[0], out[1:]

    def earlier(shift, all_x, causal_x):
        pairs = []
        for i in range(2):
            for j in range(4):
                to = (j + shift) % 4
                if i in all_x or (i in causal_x and to < j):
                    pairs.append((4 * i + j, 4 * i + to))
        return pairs

    low, high = list(pieces[:4]), list(pieces[4:])
    for j, shift in ((1, -1), (2, 1), (3, 2)):
        low[j] = lax.ppermute(low[j], BLK, earlier(shift, (1,), (0,)))
    low_sum = low[0].astype(f32) + low[1].astype(f32) + low[2].astype(f32) + low[3].astype(f32)
    across = low_sum.astype(bf16)
    high = list(gate(high, (token(across),)))
    across = lax.ppermute(across, BLK, [(i + 4, i) for i in range(4)])
    for j, shift in ((1, -1), (2, 1), (3, 2)):
        high[j] = lax.ppermute(high[j], BLK, earlier(shift, (), (1,)))
    mismatch = add_pieces(part)
    s_dk, s_dv = finish(at_x, tuple(low), across, tuple(high), (token(mismatch[:, :HD]),))
    return mismatch, s_dq, s_dk, s_dv


def solution(mesh):
    fine = Mesh(mesh.devices.reshape(2, 4, 4, 2, 2), ("xlo", "y", "z", "core", "xhi"))
    data = P(BLK, GROUP)
    flat = P(GROUP, None)
    return jax.shard_map(
        on_device,
        mesh=fine,
        in_specs=(data, data, data, flat, data, data, data, flat, P(BLK), P(BLK, None)),
        out_specs=(data, data, data, data),
        check_vma=False,
    )
```
